32 devices in a mesh: seq: 4 (over y, core), head: 8 (over z, x).
Axes of the slice: x: 2, y: 2, z: 4, core: 2. Of those that a mesh axis runs over, the one named last changes fastest.
Arguments:
- query_rows: bfloat16 [4096, 8192], P(('seq', 'head')), may hold values from -6 to 6
- key_rows: bfloat16 [4096, 1024], P(('seq', 'head')), may hold values from -6 to 6
- value_rows: bfloat16 [4096, 1024], P(('seq', 'head')), may hold values from -6 to 6
- grad_out: bfloat16 [8192, 8192], P(('seq', 'head')), may hold values from -6 to 6
- doc_ids: int32 [32], replicated, may hold values from 0 to 7, never falling along the last dimension, each value on 1 to 7 neighbouring positions
- route_table: int32 [4, 4, 4], replicated, may hold values from 0 to 8, as said below
Outputs:
- attn_out: bfloat16 [8192, 8192], P(('seq', 'head'))
- grad_query: bfloat16 [4096, 8192], P(('seq', 'head'))
- grad_key: bfloat16 [4096, 1024], P(('seq', 'head'))
- grad_value: bfloat16 [4096, 1024], P(('seq', 'head'))
The draws below stay inside these ranges and needn't reach their ends.
Inputs may be any that keep to these rules, and one draw needn't show every extreme that they name: route_table[s, t, c] is a block of sequence shard s (numbered within the shard) that seq index t takes into slot c, or 8 for an empty slot; every block of every shard appears exactly once; live slots come first in each (s, t) row; each shard fills all 4 slots for a quarter of the seq indices, 2 slots for half of them and none for the rest; one seq index has every slot live.
All inputs are finite; a program needn't handle non-finite values.
Results may differ from the reference program's by a relative error of at most 0.015.
Values may be sent and summed in bfloat16 or wider, within the bound.
No kernel may reach another device: no remote copies, remote signals or barrier semaphores. Data moves between devices by JAX's collectives and lax.ppermute only.
A program may use at most 192 MiB of HBM per device.

```python
import math
import jax
import jax.numpy as jnp
import numpy as np
from jax import lax

QH = 64
KVH = 8
DH = 128
BLOCK = 128
DOCMAX = 7
TOKENS = 4096
NB = 32
BPS = 8
CAPB = 4
N_SEQ = 4
N_HEAD = 8


def draw_query_rows(key, part):
    normal = jax.random.normal(jax.random.fold_in(key, 11), (TOKENS, QH * DH), jnp.float32)
    return jnp.clip(normal, -6.0, 6.0).astype(jnp.bfloat16)


def draw_key_rows(key, part):
    normal = jax.random.normal(jax.random.fold_in(key, 21), (TOKENS, KVH * DH), jnp.float32)
    return jnp.clip(normal, -6.0, 6.0).astype(jnp.bfloat16)


def draw_route_table(key, part):
    full_target = jax.random.randint(jax.random.fold_in(key, 31), (), 0, N_SEQ)
    source_keys = jax.random.split(jax.random.fold_in(key, 32), N_SEQ)
    order = jnp.arange(N_SEQ)
    pattern_counts = jnp.where(order < N_SEQ // 4, CAPB, jnp.where(order < 3 * N_SEQ // 4, CAPB // 2, 0)).astype(jnp.int32)

    def one_source(sub_key):
        key_blocks, key_counts = jax.random.split(sub_key)
        shuffled = jax.random.permutation(key_blocks, BPS).astype(jnp.int32)
        rest_perm = jax.random.permutation(key_counts, pattern_counts[1:])
        rest_index = jnp.clip(order - (order > full_target).astype(jnp.int32), 0, N_SEQ - 2)
        counts = jnp.where(order == full_target, CAPB, rest_perm[rest_index]).astype(jnp.int32)
        offsets = jnp.cumsum(counts) - counts
        slot_pos = jnp.arange(CAPB)
        slot_index = offsets[:, None] + slot_pos[None, :]
        is_live = slot_pos[None, :] < counts[:, None]
        return jnp.where(is_live, shuffled[jnp.clip(slot_index, 0, BPS - 1)], BPS).astype(jnp.int32)
    return jax.vmap(one_source)(source_keys).astype(jnp.int32)


def block_levels(key, shape, shards, low, top_value):
    def one(dim, shards_of):
        steps = jax.random.uniform(jax.random.fold_in(jax.random.fold_in(key, 6), dim), (shards_of,), jnp.float32, low / len(shards), top_value / len(shards))
        return jnp.repeat(jnp.exp(steps), shape[dim] // shards_of).reshape((-1,) + (1,) * (len(shape) - dim - 1))

    loudness = one(*shards[0])
    for cut in shards[1:]:
        loudness = loudness * one(*cut)
    return loudness


def split_up(amount, total, most, lean):
    loads = [(1 << 20) // math.isqrt(rank ** lean) + 1 for rank in range(2, amount + 1)]
    surplus, holding = total - most - (amount - 1), [1] * (amount - 1)
    while surplus > 0:
        movable = [i for i in range(amount - 1) if holding[i] < most]
        mass, budget = sum([loads[i] for i in movable]), surplus
        for i in movable:
            extra = min(most - holding[i], max(1, budget * loads[i] // mass), surplus)
            holding[i] = holding[i] + extra
            surplus = surplus - extra
    return np.array([most] + holding)


def uneven(own_key, count, total, reach, lean):
    if count == 2:
        one = jax.random.randint(own_key, (), max(1, total - reach), min(reach, total - 1) + 1)
        return jnp.stack([one, total - one])
    tallies = jnp.asarray(split_up(count, total, reach, lean), jnp.int32)
    twos = (count - 1) // 2
    source_of, receiver = tallies[1:1 + 2 * twos:2], tallies[2:2 + 2 * twos:2]
    room = jnp.minimum(source_of - 1, reach - receiver)
    moved = jax.random.randint(jax.random.fold_in(own_key, 1), (twos,), 0, 1 << 20) % (room + 1)
    tallies = tallies.at[1:1 + 2 * twos:2].set(source_of - moved).at[2:2 + 2 * twos:2].set(receiver + moved)
    return tallies[jax.random.permutation(jax.random.fold_in(own_key, 2), count)]


def normal_values(own_key, shape, deviation, most, cuts=(), held_as=jnp.bfloat16):
    loudness = block_levels(own_key, shape, cuts, -0.22, 0.18) if cuts else 1.0
    array = jax.random.normal(own_key, shape, jnp.float32) * deviation * loudness
    return jnp.minimum(jnp.maximum(array, -most), most).astype(held_as)


def setup_inputs(seed: int = 0) -> dict:
    arg_keys = jax.random.split(jax.random.key(seed), 7)
    return {
        "query_rows": draw_query_rows(jax.random.fold_in(arg_keys[6], 71), 0),
        "key_rows": draw_key_rows(jax.random.fold_in(arg_keys[6], 71), 0),
        "value_rows": normal_values(arg_keys[2], (TOKENS, KVH * DH), 1.0, 6.0, ((0, 32),)),
        "grad_out": normal_values(arg_keys[3], (2 * TOKENS, QH * DH), 1.0, 6.0, ((0, 32),)),
        "doc_ids": jnp.searchsorted(jnp.cumsum(uneven(arg_keys[4], NB // 4, NB, DOCMAX, 2)), jnp.arange(NB), side="right").astype(jnp.int32),
        "route_table": draw_route_table(jax.random.fold_in(arg_keys[6], 71), 0),
    }


def slot_math(queries, cotangent, keys_win, values_win, allowed, alive_flag, factor):
    query_wide = queries.astype(jnp.float32)
    key_wide = keys_win.astype(jnp.float32)
    value_wide = values_win.astype(jnp.float32)
    scores = jnp.einsum('hpbd,hnd->hpbn', query_wide, key_wide) * factor
    scores = jnp.where(allowed[None, None], scores, -jnp.inf)
    rowmax = lax.optimization_barrier(jnp.max(scores, axis=-1, keepdims=True))
    exponent = jnp.where(allowed[None, None], jnp.exp(scores - rowmax), jnp.zeros_like(scores))
    weights = exponent / lax.optimization_barrier(jnp.sum(exponent, axis=-1, keepdims=True))
    weights_b = lax.optimization_barrier(weights.astype(jnp.bfloat16)).astype(jnp.float32)
    output = jnp.einsum('hpbn,hnd->hpbd', weights_b, value_wide)
    output = jnp.where(alive_flag, output, jnp.zeros_like(output))
    output_b = lax.optimization_barrier(output.astype(jnp.bfloat16))
    output_wide = output_b.astype(jnp.float32)
    cot_wide = cotangent.astype(jnp.float32)
    cot_wide = jnp.where(alive_flag, cot_wide, jnp.zeros_like(cot_wide))
    deltas = lax.optimization_barrier(jnp.sum(cot_wide * output_wide, axis=-1, keepdims=True))
    prob_grad = jnp.einsum('hpbd,hnd->hpbn', cot_wide, value_wide)
    dscore = lax.optimization_barrier((weights * (prob_grad - deltas) * factor).astype(jnp.bfloat16)).astype(jnp.float32)
    grad_rows = jnp.einsum('hpbn,hnd->hpbd', dscore, key_wide).astype(jnp.bfloat16)
    key_part = jnp.einsum('hpbn,hpbd->hnd', dscore, query_wide)
    value_part = jnp.einsum('hpbn,hpbd->hnd', weights_b, cot_wide)
    return (output_b, grad_rows, key_part, value_part)

def reference(query_rows, key_rows, value_rows, grad_out, doc_ids, route_table):
    per_dev = QH // N_HEAD
    repeats = N_HEAD // KVH
    slot_total = N_SEQ * CAPB
    window = DOCMAX * BLOCK
    margin = (DOCMAX - 1) * BLOCK
    factor = 1.0 / math.sqrt(DH)
    key_pad = jnp.concatenate([jnp.zeros((margin, KVH * DH), key_rows.dtype), key_rows], axis=0)
    value_pad = jnp.concatenate([jnp.zeros((margin, KVH * DH), value_rows.dtype), value_rows], axis=0)
    doc_pad = jnp.concatenate([jnp.full((DOCMAX - 1,), -1, jnp.int32), doc_ids.astype(jnp.int32)])
    columns = jnp.arange(window)
    row_pos = jnp.arange(BLOCK)
    causal = (columns[None, :] < margin) | (columns[None, :] - margin <= row_pos[:, None])
    source = jnp.repeat(jnp.arange(N_SEQ, dtype=jnp.int32), CAPB)
    grad_store = jnp.zeros((NB + 1, BLOCK, QH * DH), jnp.bfloat16)
    key_total = jnp.zeros((N_HEAD, TOKENS, 2 * DH), jnp.float32)
    out_parts = []
    for target in range(N_SEQ):
        recv_index = route_table[:, target, :].reshape(-1).astype(jnp.int32)
        alive_all = recv_index < BPS
        block_ids = jnp.where(alive_all, source * BPS + recv_index, 0).astype(jnp.int32)
        store_ids = jnp.where(alive_all, block_ids, NB).astype(jnp.int32)

        def slot_step(partial_value, slot, target=target, block_ids=block_ids, alive_all=alive_all):
            block_id = block_ids[slot].astype(jnp.int32)
            alive_flag = alive_all[slot]
            row_first = (block_id * BLOCK).astype(jnp.int32)
            queries = lax.dynamic_slice_in_dim(query_rows, row_first, BLOCK, 0)
            queries = queries.reshape(BLOCK, N_HEAD, per_dev, DH).transpose(1, 2, 0, 3)
            row_start = ((target * slot_total + slot) * BLOCK).astype(jnp.int32)
            cotangent = lax.dynamic_slice_in_dim(grad_out, row_start, BLOCK, 0)
            cotangent = cotangent.reshape(BLOCK, N_HEAD, per_dev, DH).transpose(1, 2, 0, 3)
            keys_win = lax.dynamic_slice_in_dim(key_pad, row_first, window, 0).reshape(window, KVH, DH).transpose(1, 0, 2)
            keys_win = jnp.repeat(keys_win, repeats, axis=0)
            values_win = lax.dynamic_slice_in_dim(value_pad, row_first, window, 0).reshape(window, KVH, DH).transpose(1, 0, 2)
            values_win = jnp.repeat(values_win, repeats, axis=0)
            docs_win = lax.dynamic_slice_in_dim(doc_pad, block_id, DOCMAX, 0)
            same_doc = jnp.repeat(docs_win == docs_win[DOCMAX - 1], BLOCK)
            allowed = causal & same_doc[None, :]
            output, grad_rows, key_part, value_part = slot_math(queries, cotangent, keys_win, values_win, allowed, alive_flag, factor)
            update = jnp.concatenate([key_part, value_part], axis=-1)
            current = lax.dynamic_slice_in_dim(partial_value, row_first, window, 1)
            partial_value = lax.dynamic_update_slice_in_dim(partial_value, current + update, row_first, 1)
            return (partial_value, (output, grad_rows))
        partial_init = jnp.zeros((N_HEAD, margin + TOKENS, 2 * DH), jnp.float32)
        partial_value, (outputs, grad_rows) = lax.scan(slot_step, partial_init, jnp.arange(slot_total, dtype=jnp.int32))
        out_parts.append(outputs.transpose(0, 3, 1, 2, 4).reshape(slot_total * BLOCK, QH * DH))
        grad_blocks = grad_rows.transpose(0, 3, 1, 2, 4).reshape(slot_total, BLOCK, QH * DH)
        grad_store = grad_store.at[store_ids].set(grad_blocks)
        rounded = lax.optimization_barrier(partial_value[:, margin:].astype(jnp.bfloat16)).astype(jnp.float32)
        key_total = key_total + rounded
    attn_out = jnp.concatenate(out_parts, axis=0)
    grad_query = grad_store[:NB].reshape(TOKENS, QH * DH)
    group_wide = lax.optimization_barrier(key_total.astype(jnp.bfloat16)).astype(jnp.float32)
    group_sum = lax.optimization_barrier(jnp.sum(group_wide.reshape(KVH, repeats, TOKENS, 2 * DH), axis=1)).astype(jnp.bfloat16)
    grad_key = group_sum[:, :, :DH].transpose(1, 0, 2).reshape(TOKENS, KVH * DH)
    grad_value = group_sum[:, :, DH:].transpose(1, 0, 2).reshape(TOKENS, KVH * DH)
    return (attn_out, grad_query, grad_key, grad_value)
```

```python
import functools
import math

import jax
import jax.numpy as jnp
from jax import lax
from jax.experimental import pallas as pl
from jax.experimental.pallas import tpu as pltpu
from jax.sharding import Mesh
from jax.sharding import PartitionSpec as P

QH = 64
KVH = 8
DH = 128
BLOCK = 128
DOCMAX = 7
HALO = DOCMAX - 1
CHUNKS = 2

ANY = pl.BlockSpec(memory_space=pl.ANY)
NT = (((1,), (1,)), ((), ()))
F32 = jnp.float32
BF16 = jnp.bfloat16


def pack_query(query_rows, key_rows, value_rows, groups):
    width = QH // groups * DH
    half = width // CHUNKS
    repeats = groups // KVH

    def kernel(q_ref, k_ref, v_ref, first_ref, second_ref):
        first_ref[0, :, :half] = q_ref[:, :half]
        first_ref[0, :, half : half + DH] = k_ref[...]
        first_ref[0, :, half + DH :] = v_ref[...]
        second_ref[0] = q_ref[:, half:]

    return pl.pallas_call(
        kernel,
        grid=(groups,),
        in_specs=[
            pl.BlockSpec((BLOCK, width), lambda r: (0, r)),
            pl.BlockSpec((BLOCK, DH), lambda r: (0, r // repeats)),
            pl.BlockSpec((BLOCK, DH), lambda r: (0, r // repeats)),
        ],
        out_specs=[
            pl.BlockSpec((1, BLOCK, half + 2 * DH), lambda r: (r, 0, 0)),
            pl.BlockSpec((1, BLOCK, half), lambda r: (r, 0, 0)),
        ],
        out_shape=[
            jax.ShapeDtypeStruct((groups, BLOCK, half + 2 * DH), BF16),
            jax.ShapeDtypeStruct((groups, BLOCK, half), BF16),
        ],
        name="pack_query",
    )(query_rows, key_rows, value_rows)


def pack_grad(grad_out, groups):
    rows = grad_out.shape[0]
    width = QH // groups * DH
    half = width // CHUNKS

    def kernel(g_ref, first_ref, second_ref):
        first_ref[0] = g_ref[:, :half]
        second_ref[0] = g_ref[:, half:]

    return pl.pallas_call(
        kernel,
        grid=(groups,),
        in_specs=[pl.BlockSpec((rows, width), lambda r: (0, r))],
        out_specs=[pl.BlockSpec((1, rows, half), lambda r: (r, 0, 0))] * 2,
        out_shape=[jax.ShapeDtypeStruct((groups, rows, half), BF16)] * 2,
        name="pack_grad",
    )(grad_out)


def attend(table, kv_parts, halo_parts, query_parts, grad_slots, carried, last, shard_blocks):
    n_src = len(kv_parts)
    per_src = kv_parts[0].shape[0]
    blocks = shard_blocks
    width = grad_slots.shape[-1]
    slots = grad_slots.shape[0]
    base = blocks - HALO
    span = blocks + HALO
    pairs = width // (2 * DH)
    scale = 1.0 / math.sqrt(DH)
    exponent = scale * math.log2(math.e)
    first = carried is None
    out_width = width + 2 * DH if last else width

    def kernel(*refs):
        refs = list(refs)
        tab = refs.pop(0)
        kv_refs = [refs.pop(0) for _ in range(n_src)]
        halo_refs = [refs.pop(0) for _ in range(n_src)]
        q_refs = kv_refs if first else [refs.pop(0) for _ in range(n_src)]
        go_ref = refs.pop(0)
        carried_ref = None if first else refs.pop(0)
        out_ref = refs.pop(0)
        gq_refs = [refs.pop(0) for _ in range(blocks)]
        if last:
            back_refs = [refs.pop(0) for _ in range(blocks)]
        else:
            acc_out = refs.pop(0)
        qs, gs, kvs, kts, vts, acc, os, gqs, zero, sem_in, sem_go, sem_out, sem_end = refs[:13]
        if last:
            backs = refs[13]
        plane = tab[2 * blocks]
        core = tab[2 * blocks + 1]

        loads = []

        def load(src, dst):
            copy = pltpu.make_async_copy(src, dst, sem_in.at[len(loads)])
            copy.start()
            loads.append(copy)

        for k in range(n_src):
            at = (plane ^ k) * per_src
            load(kv_refs[k].at[:, :, kv_refs[k].shape[-1] - 2 * DH :], kvs.at[pl.ds(blocks + at, per_src)])
            load(halo_refs[k], kvs.at[pl.ds(at, per_src)])
            load(q_refs[k].at[:, :, :width], qs.at[pl.ds(at, per_src)])
        if not first:
            load(carried_ref, acc)

        def go_copy(i):
            return pltpu.make_async_copy(go_ref.at[tab[i]], gs.at[i], sem_go.at[i])

        def out_copy(i):
            return pltpu.make_async_copy(os.at[i], out_ref.at[tab[i]], sem_out.at[i])

        @pl.loop(0, blocks)
        def _(i):
            go_copy(i).start()

        zero[...] = jnp.zeros_like(zero)
        for slot in range(slots):
            @pl.when(tab[2 * blocks + 2 + slot] == 0)
            def _():
                pltpu.make_async_copy(zero, out_ref.at[slot], sem_end.at[slot]).start()

        if first:
            acc[...] = jnp.zeros_like(acc)
        for copy in loads:
            copy.wait()

        @pl.loop(0, span)
        def _(b):
            at = pl.multiple_of(b * DH, DH)
            kts[:, pl.ds(at, DH)] = kvs[base + b, :, :DH].T
            vts[:, pl.ds(at, DH)] = kvs[base + b, :, DH:].T

        key_at = lax.broadcasted_iota(jnp.int32, (BLOCK, 2 * BLOCK), 0)
        query_at = lax.broadcasted_iota(jnp.int32, (BLOCK, 2 * BLOCK), 1) % BLOCK
        causal = key_at <= query_at

        def block_body(n, i, k):
            start = blocks + i - (n - 1)
            rel = HALO + i - (n - 1)
            size = n * BLOCK
            keys = kvs[pl.ds(start, n), :, :DH].reshape(size, DH)
            values = kvs[pl.ds(start, n), :, DH:].reshape(size, DH)
            lane = pl.multiple_of(rel * DH, DH)
            keys_t = kts[:, pl.ds(lane, size)]
            values_t = vts[:, pl.ds(lane, size)]
            for pair in range(pairs):
                c0 = pair * 2 * DH
                q2 = jnp.concatenate([qs[i, :, c0 : c0 + DH], qs[i, :, c0 + DH : c0 + 2 * DH]], axis=0)
                g2 = jnp.concatenate([gs[i, :, c0 : c0 + DH], gs[i, :, c0 + DH : c0 + 2 * DH]], axis=0)
                s = lax.dot_general(keys, q2, NT, preferred_element_type=F32)
                diag = jnp.where(causal, s[size - BLOCK :], -jnp.inf)
                s = jnp.concatenate([s[: size - BLOCK], diag], axis=0) if n > 1 else diag
                top = jnp.max(s, axis=0, keepdims=True)
                p = jnp.exp2((s - top) * exponent)
                w = p * (1.0 / jnp.sum(p, axis=0, keepdims=True))
                wb = w.astype(BF16)
                o_t = jnp.dot(values_t, wb, preferred_element_type=F32)
                dp = lax.dot_general(values, g2, NT, preferred_element_type=F32)
                delta = jnp.sum(w * dp, axis=0, keepdims=True)
                ds = (w * (dp - delta)).astype(BF16)
                dq_t = jnp.dot(keys_t, ds, preferred_element_type=F32) * scale
                dk = jnp.dot(ds, q2, preferred_element_type=F32)
                dv = jnp.dot(wb, g2, preferred_element_type=F32)
                acc[pl.ds(rel, n), :, :DH] += dk.reshape(n, BLOCK, DH)
                acc[pl.ds(rel, n), :, DH:] += dv.reshape(n, BLOCK, DH)
                for side in range(2):
                    c1 = c0 + side * DH
                    os[i, :, c1 : c1 + DH] = o_t[:, side * BLOCK : (side + 1) * BLOCK].T.astype(BF16)
                    gqs[k, :, c1 : c1 + DH] = dq_t[:, side * BLOCK : (side + 1) * BLOCK].T.astype(BF16)

        @pl.loop(0, blocks)
        def _(k):
            i = core ^ k
            go_copy(i).wait()
            count = tab[blocks + i]
            for n in range(1, DOCMAX + 1):
                @pl.when(count == n)
                def _():
                    block_body(n, i, k)
            out_copy(i).start()

        if last:
            @pl.loop(0, blocks)
            def _(k):
                i = core ^ k
                gqs[k, :, width : width + DH] = (acc[HALO + i, :, :DH] * scale).astype(BF16)
                gqs[k, :, width + DH :] = acc[HALO + i, :, DH:].astype(BF16)
                near = jnp.maximum(i - base, 0)
                backs[k, :, :DH] = (acc[near, :, :DH] * scale).astype(BF16)
                backs[k, :, DH:] = acc[near, :, DH:].astype(BF16)

        stores = []

        def store(src, dst):
            copy = pltpu.make_async_copy(src, dst, sem_end.at[slots + len(stores)])
            copy.start()
            stores.append(copy)

        for k in range(blocks):
            store(gqs.at[k], gq_refs[k])
            if last:
                store(backs.at[k], back_refs[k])
        if not last:
            store(acc, acc_out)

        for copy in stores:
            copy.wait()

        @pl.loop(0, blocks)
        def _(i):
            out_copy(i).wait()

        for slot in range(slots):
            @pl.when(tab[2 * blocks + 2 + slot] == 0)
            def _():
                pltpu.make_async_copy(zero, out_ref.at[slot], sem_end.at[slot]).wait()

    operands = [table, *kv_parts, *halo_parts]
    if not first:
        operands += query_parts
    operands.append(grad_slots)
    if not first:
        operands.append(carried)
    out_shape = [jax.ShapeDtypeStruct((slots, BLOCK, width), BF16)]
    out_shape += [jax.ShapeDtypeStruct((BLOCK, out_width), BF16)] * blocks
    if last:
        out_shape += [jax.ShapeDtypeStruct((BLOCK, 2 * DH), BF16)] * blocks
    else:
        out_shape += [jax.ShapeDtypeStruct((span, BLOCK, 2 * DH), F32)]
    scratch = [
        pltpu.VMEM((blocks, BLOCK, width), BF16),
        pltpu.VMEM((blocks, BLOCK, width), BF16),
        pltpu.VMEM((2 * blocks, BLOCK, 2 * DH), BF16),
        pltpu.VMEM((DH, span * BLOCK), BF16),
        pltpu.VMEM((DH, span * BLOCK), BF16),
        pltpu.VMEM((span, BLOCK, 2 * DH), F32),
        pltpu.VMEM((blocks, BLOCK, width), BF16),
        pltpu.VMEM((blocks, BLOCK, out_width), BF16),
        pltpu.VMEM((BLOCK, width), BF16),
        pltpu.SemaphoreType.DMA((3 * n_src + 1,)),
        pltpu.SemaphoreType.DMA((blocks,)),
        pltpu.SemaphoreType.DMA((blocks,)),
        pltpu.SemaphoreType.DMA((slots + 2 * blocks + 1,)),
    ]
    if last:
        scratch.append(pltpu.VMEM((blocks, BLOCK, 2 * DH), BF16))
    work = blocks * width // DH * 4
    results = pl.pallas_call(
        kernel,
        in_specs=[pl.BlockSpec(memory_space=pltpu.SMEM)] + [ANY] * (len(operands) - 1),
        out_specs=[ANY] * len(out_shape),
        out_shape=out_shape,
        scratch_shapes=scratch,
        cost_estimate=pl.CostEstimate(
            flops=work * 10 * BLOCK**3, bytes_accessed=12 << 20, transcendentals=work * BLOCK**2
        ),
        compiler_params=pltpu.CompilerParams(vmem_limit_bytes=48 << 20),
        name="attend_last" if last else "attend_first",
    )(*operands)
    out = results[0]
    rows = results[1 : 1 + blocks]
    return out, rows, results[1 + blocks :]


def place_rows(block_index, first_rows, last_rows, backs, groups):
    repeats = groups // KVH
    width = QH // groups * DH
    half = width // CHUNKS

    def kernel(*refs):
        refs = list(refs)
        at = refs.pop(0)[0]
        firsts = [refs.pop(0) for _ in range(groups)]
        lasts = [refs.pop(0) for _ in range(groups)]
        terms = [refs.pop(0) for _ in range(groups)]
        gq_ref, gk_ref, gv_ref, keys, values = refs
        for k in range(groups):
            group = at ^ k
            col = pl.multiple_of(group * width, width)
            gq_ref[:, pl.ds(col, half)] = firsts[k][...]
            gq_ref[:, pl.ds(pl.multiple_of(col + half, half), half)] = lasts[k][:, :half]
            keys[group] = lasts[k][:, half : half + DH].astype(F32) + terms[k][:, :DH].astype(F32)
            values[group] = lasts[k][:, half + DH :].astype(F32) + terms[k][:, DH:].astype(F32)
        for head in range(KVH):
            key_sum, value_sum = keys[head * repeats], values[head * repeats]
            for extra in range(1, repeats):
                key_sum += keys[head * repeats + extra]
                value_sum += values[head * repeats + extra]
            gk_ref[:, head * DH : (head + 1) * DH] = key_sum.astype(BF16)
            gv_ref[:, head * DH : (head + 1) * DH] = value_sum.astype(BF16)

    vmem = pl.BlockSpec(memory_space=pltpu.VMEM)
    return pl.pallas_call(
        kernel,
        in_specs=[pl.BlockSpec(memory_space=pltpu.SMEM)] + [vmem] * (3 * groups),
        out_specs=[vmem] * 3,
        out_shape=[
            jax.ShapeDtypeStruct((BLOCK, QH * DH), BF16),
            jax.ShapeDtypeStruct((BLOCK, KVH * DH), BF16),
            jax.ShapeDtypeStruct((BLOCK, KVH * DH), BF16),
        ],
        scratch_shapes=[pltpu.VMEM((groups, BLOCK, DH), F32)] * 2,
        name="place_rows",
    )(block_index, *first_rows, *last_rows, *backs)


def place_out(first, last):
    groups, rows, half = first.shape

    def kernel(first_ref, last_ref, out_ref):
        out_ref[:, :half] = first_ref[0]
        out_ref[:, half:] = last_ref[0]

    spec = pl.BlockSpec((1, rows, half), lambda r: (r, 0, 0))
    return pl.pallas_call(
        kernel,
        grid=(groups,),
        in_specs=[spec, spec],
        out_specs=pl.BlockSpec((rows, 2 * half), lambda r: (0, r)),
        out_shape=jax.ShapeDtypeStruct((rows, QH * DH), BF16),
        name="place_out",
    )(first, last)


def body(shape, query_rows, key_rows, value_rows, grad_out, doc_ids, route_table):
    n_seq, n_plane, per_plane = shape
    groups = n_seq * per_plane
    blocks = n_plane * per_plane
    slots = route_table.shape[1] * route_table.shape[2]
    axes = ("seq", "hs", "hp")
    plane_axes = ("seq", "hp")
    seq_at = lax.axis_index("seq")
    plane = lax.axis_index("hs")
    part = lax.axis_index("hp")
    core = seq_at * per_plane + part
    near = (blocks - HALO) // per_plane

    def device(seq, hs, hp):
        return (seq * n_plane + hs) * per_plane + hp

    every = [(a, b, c) for a in range(n_seq) for b in range(n_plane) for c in range(per_plane)]

    def swap(x):
        return lax.all_to_all(x, plane_axes, split_axis=0, concat_axis=0, tiled=True)

    def along(x, k, keep):
        pairs = [(device(a, b, c), device(a, b ^ k, c)) for a, b, c in every if keep(b, b ^ k)]
        return lax.ppermute(x, axes, pairs)

    def home(x, k, shift):
        pairs = []
        for a, b, c in every:
            index = (a * per_plane + c) ^ k
            if b >= shift and (shift == 0 or index >= blocks - HALO):
                pairs.append(
                    (device(a, b, c), device(b - shift, index // per_plane, index % per_plane))
                )
        return lax.ppermute(x, axes, pairs)

    routes = lax.dynamic_index_in_dim(route_table, plane, 0, keepdims=False).reshape(slots)
    match = routes[None, :] == jnp.arange(blocks, dtype=jnp.int32)[:, None]
    slot_of = jnp.sum(jnp.where(match, jnp.arange(slots, dtype=jnp.int32)[None, :], 0), axis=1)
    docs_pad = jnp.concatenate([jnp.full((HALO,), -1, jnp.int32), doc_ids])
    docs = lax.dynamic_slice_in_dim(docs_pad, plane * blocks, blocks + HALO, 0)
    own = docs[HALO:]
    counts = sum((docs[HALO - d : HALO - d + blocks] == own).astype(jnp.int32) for d in range(DOCMAX))
    live = (routes < blocks).astype(jnp.int32)
    table = jnp.concatenate(
        [slot_of, counts, jnp.stack([plane, core]).astype(jnp.int32), live]
    )

    first_pack, second_pack = pack_query(query_rows, key_rows, value_rows, groups)
    grad_first, grad_second = pack_grad(grad_out, groups)
    width = grad_first.shape[-1]

    def spread(x):
        return x.reshape((n_seq, per_plane) + x.shape[1:])

    def piece(x, index):
        return lax.dynamic_index_in_dim(x, index, 0, keepdims=False)

    first_plane = spread(swap(first_pack))
    kv_parts, halo_parts, query_parts = [], [], []
    for k in range(n_plane):
        part_k = piece(first_plane, plane ^ k)
        kv_parts.append(along(part_k, k, lambda b, d: True) if k else part_k)
    for k in range(n_plane):
        part_k = piece(first_plane[..., width:], jnp.maximum((plane ^ k) - 1, 0))
        halo_parts.append(along(part_k, k, lambda b, d: b >= near and d >= 1) if k else part_k)
    second_plane = spread(swap(second_pack))
    for k in range(n_plane):
        part_k = piece(second_plane, plane ^ k)
        query_parts.append(along(part_k, k, lambda b, d: True) if k else part_k)

    def by_slot(x):
        return swap(x).reshape(slots, BLOCK, width)

    out_first, rows_first, (carried,) = attend(
        table, kv_parts, halo_parts, None, by_slot(grad_first), None, False, blocks
    )
    home_first = [home(rows_first[k], k, 0) for k in range(blocks)]
    back_first = swap(out_first.reshape(groups, -1, width))
    out_second, rows_second, backs = attend(
        table, kv_parts, halo_parts, query_parts, by_slot(grad_second), carried, True, blocks
    )
    home_second = [home(rows_second[k], k, 0) for k in range(blocks)]
    home_backs = [home(backs[k], k, 1) for k in range(blocks)]
    back_second = swap(out_second.reshape(groups, -1, width))

    block_index = (plane * per_plane + part).astype(jnp.int32).reshape(1)
    grad_query, grad_key, grad_value = place_rows(
        block_index, home_first, home_second, home_backs, groups
    )
    attn_out = place_out(back_first, back_second)
    return (attn_out, grad_query, grad_key, grad_value)


def solution(mesh):
    n_seq, n_head = mesh.shape["seq"], mesh.shape["head"]
    per_plane = n_head // n_seq
    shape = (n_seq, n_seq, per_plane)
    wide = Mesh(mesh.devices.reshape(shape), ("seq", "hs", "hp"))
    rows = P(("seq", "hs", "hp"), None)
    return jax.shard_map(
        functools.partial(body, shape),
        mesh=wide,
        in_specs=(rows, rows, rows, rows, P(), P()),
        out_specs=(rows, rows, rows, rows),
        check_vma=False,
    )
```

```python
import functools
import math

import jax
import jax.numpy as jnp
from jax import lax
from jax.experimental import pallas as pl
from jax.experimental.pallas import tpu as pltpu
from jax.sharding import Mesh
from jax.sharding import PartitionSpec as P


QH = 64
KVH = 8
DH = 128
BLOCK = 128
DOCMAX = 7
HALO = DOCMAX - 1
CHUNKS = 2

ANY = pl.BlockSpec(memory_space=pl.ANY)
NT = (((1,), (1,)), ((), ()))
F32 = jnp.float32
BF16 = jnp.bfloat16


def pack(sources, groups):
    count = sources[0][0].shape[0]
    total = sum(width for _, width, _ in sources)

    def kernel(*refs):
        ins, out_ref, held, sem_in, sem_out = refs[: len(sources)], *refs[len(sources) :]
        loads, stores = [], []
        for r in range(groups):
            at = 0
            for n, (_, width, index) in enumerate(sources):
                col = index(r) * width
                copy = pltpu.make_async_copy(
                    ins[n].at[:, col : col + width],
                    held.at[r, :, at : at + width],
                    sem_in.at[r * len(sources) + n],
                )
                copy.start()
                loads.append(copy)
                at += width
        for r in range(groups):
            for n in range(len(sources)):
                loads[r * len(sources) + n].wait()
            copy = pltpu.make_async_copy(held.at[r], out_ref.at[r], sem_out.at[r])
            copy.start()
            stores.append(copy)
        for copy in stores:
            copy.wait()

    return pl.pallas_call(
        kernel,
        in_specs=[ANY] * len(sources),
        out_specs=ANY,
        out_shape=jax.ShapeDtypeStruct((groups, count, total), BF16),
        scratch_shapes=[
            pltpu.VMEM((groups, count, total), BF16),
            pltpu.SemaphoreType.DMA((groups * len(sources),)),
            pltpu.SemaphoreType.DMA((groups,)),
        ],
        cost_estimate=pl.CostEstimate(
            flops=0, bytes_accessed=4 * groups * count * total, transcendentals=0
        ),
        compiler_params=pltpu.CompilerParams(vmem_limit_bytes=62 << 20),
    )(*[rows for rows, _, _ in sources])


def pack_first(query_rows, key_rows, value_rows, groups):
    width = QH // groups * DH
    repeats = groups // KVH
    sources = [
        (query_rows, width, lambda r: r),
        (key_rows, DH, lambda r: r // repeats),
        (value_rows, DH, lambda r: r // repeats),
    ]
    return pack(sources, groups)


def pack_half(rows, chunk, groups):
    half = QH // groups * DH // CHUNKS
    return pack([(rows, half, lambda r: r * CHUNKS + chunk)], groups)


def relay_in(plane_index, arrived, width):
    n_plane, per_plane = arrived.shape[:2]
    kv = 2 * DH

    def kernel(plane_ref, in_ref, *refs):
        firsts, refs = refs[:n_plane], refs[n_plane:]
        seconds, (one, two, sem_in, sem_out) = refs[:n_plane], refs[n_plane:]
        loads, stores = [], []
        for k in range(n_plane):
            to = plane_ref[0] ^ k
            near = jnp.maximum(to - 1, 0)
            views = [
                (in_ref.at[to, :, :, :width], one.at[k, :, :, :width]),
                (in_ref.at[to, :, :, 2 * width :], one.at[k, :, :, width : width + kv]),
                (in_ref.at[near, :, :, 2 * width :], one.at[k, :, :, width + kv :]),
                (in_ref.at[to, :, :, width : 2 * width], two.at[k]),
            ]
            for n, (src, dst) in enumerate(views):
                copy = pltpu.make_async_copy(src, dst, sem_in.at[4 * k + n])
                copy.start()
                loads.append(copy)
        for k in range(n_plane):
            for copy in loads[4 * k : 4 * k + 4]:
                copy.wait()
            for n, (src, dst) in enumerate(((one.at[k], firsts[k]), (two.at[k], seconds[k]))):
                copy = pltpu.make_async_copy(src, dst, sem_out.at[2 * k + n])
                copy.start()
                stores.append(copy)
        for copy in stores:
            copy.wait()

    one = (per_plane, BLOCK, width + 2 * kv)
    two = (per_plane, BLOCK, width)
    results = pl.pallas_call(
        kernel,
        in_specs=[pl.BlockSpec(memory_space=pltpu.SMEM), ANY],
        out_specs=[ANY] * (2 * n_plane),
        out_shape=[jax.ShapeDtypeStruct(one, BF16)] * n_plane
        + [jax.ShapeDtypeStruct(two, BF16)] * n_plane,
        scratch_shapes=[
            pltpu.VMEM((n_plane, *one), BF16),
            pltpu.VMEM((n_plane, *two), BF16),
            pltpu.SemaphoreType.DMA((4 * n_plane,)),
            pltpu.SemaphoreType.DMA((2 * n_plane,)),
        ],
        cost_estimate=pl.CostEstimate(flops=0, bytes_accessed=6 << 20, transcendentals=0),
        compiler_params=pltpu.CompilerParams(vmem_limit_bytes=62 << 20),
        name="relay_in",
    )(plane_index, arrived)
    return list(results[:n_plane]), list(results[n_plane:])


def relay_out(plane_index, parts, held):
    n_plane = len(parts)
    per_plane, _, width = parts[0].shape
    first_row = held.shape[1] - BLOCK

    def kernel(plane_ref, *refs):
        ins, (_, out_ref, buf, sem_in, sem_out) = refs[:n_plane], refs[n_plane:]
        loads, stores = [], []
        for k in range(n_plane):
            copy = pltpu.make_async_copy(ins[k], buf.at[k], sem_in.at[k])
            copy.start()
            loads.append(copy)
        for k in range(n_plane):
            loads[k].wait()
            at = (plane_ref[0] ^ k) * per_plane
            copy = pltpu.make_async_copy(
                buf.at[k], out_ref.at[pl.ds(at, per_plane), first_row:, :], sem_out.at[k]
            )
            copy.start()
            stores.append(copy)
        for copy in stores:
            copy.wait()

    return pl.pallas_call(
        kernel,
        in_specs=[pl.BlockSpec(memory_space=pltpu.SMEM)] + [ANY] * (n_plane + 1),
        out_specs=ANY,
        out_shape=jax.ShapeDtypeStruct(held.shape, BF16),
        scratch_shapes=[
            pltpu.VMEM((n_plane, per_plane, BLOCK, width), BF16),
            pltpu.SemaphoreType.DMA((n_plane,)),
            pltpu.SemaphoreType.DMA((n_plane,)),
        ],
        input_output_aliases={n_plane + 1: 0},
        cost_estimate=pl.CostEstimate(flops=0, bytes_accessed=2 << 20, transcendentals=0),
        compiler_params=pltpu.CompilerParams(vmem_limit_bytes=62 << 20),
        name="relay_out",
    )(plane_index, *parts, held)


def attend(table, kv_parts, query_parts, grad_slots, carried, last, shard_blocks, out_form):
    n_src = len(kv_parts)
    per_src = kv_parts[0].shape[0]
    blocks = shard_blocks
    width = grad_slots.shape[-1]
    slots = grad_slots.shape[0]
    per_core = slots // out_form[0]
    base = blocks - HALO
    span = blocks + HALO
    pairs = width // (2 * DH)
    scale = 1.0 / math.sqrt(DH)
    exponent = scale * math.log2(math.e)
    first = carried is None

    def kernel(*refs):
        refs = list(refs)
        tab = refs.pop(0)
        kv_refs = [refs.pop(0) for _ in range(n_src)]
        q_refs = kv_refs if first else [refs.pop(0) for _ in range(n_src)]
        go_ref = refs.pop(0)
        carried_ref = None if first else refs.pop(0)
        out_ref = refs.pop(0)
        if last:
            gq_ref, main_ref, back_ref = refs.pop(0), refs.pop(0), refs.pop(0)
        else:
            gq_refs = [refs.pop(0) for _ in range(n_src)]
            acc_out = refs.pop(0)
        qs, gs, kvs, kts, vts, acc, os, gqs, zero, sem_in, sem_go, sem_out, sem_end = refs[:13]
        if last:
            backs = refs[13]
        plane = tab[2 * blocks]
        core = tab[2 * blocks + 1]

        loads = []

        def load(src, dst):
            copy = pltpu.make_async_copy(src, dst, sem_in.at[len(loads)])
            copy.start()
            loads.append(copy)

        for k in range(n_src):
            at = (plane ^ k) * per_src
            load(kv_refs[k].at[:, :, width : width + 2 * DH], kvs.at[pl.ds(blocks + at, per_src)])
            load(kv_refs[k].at[:, :, width + 2 * DH :], kvs.at[pl.ds(at, per_src)])
            load(q_refs[k].at[:, :, :width], qs.at[pl.ds(at, per_src)])
        if not first:
            load(carried_ref, acc)

        def slot_ref(slot):
            row = pl.multiple_of(slot % per_core * BLOCK, BLOCK)
            return out_ref.at[slot // per_core, pl.ds(row, BLOCK), :]

        def go_copy(i):
            return pltpu.make_async_copy(go_ref.at[tab[i]], gs.at[i], sem_go.at[i])

        def out_copy(i):
            return pltpu.make_async_copy(os.at[i], slot_ref(tab[i]), sem_out.at[i])

        @pl.loop(0, blocks)
        def _(i):
            go_copy(i).start()

        zero[...] = jnp.zeros_like(zero)
        for slot in range(slots):
            @pl.when(tab[2 * blocks + 2 + slot] == 0)
            def _():
                pltpu.make_async_copy(zero, slot_ref(slot), sem_end.at[slot]).start()

        if first:
            acc[...] = jnp.zeros_like(acc)
        for copy in loads:
            copy.wait()

        @pl.loop(0, span)
        def _(b):
            at = pl.multiple_of(b * DH, DH)
            kts[:, pl.ds(at, DH)] = kvs[base + b, :, :DH].T
            vts[:, pl.ds(at, DH)] = kvs[base + b, :, DH:].T

        key_at = lax.broadcasted_iota(jnp.int32, (BLOCK, 2 * BLOCK), 0)
        query_at = lax.broadcasted_iota(jnp.int32, (BLOCK, 2 * BLOCK), 1) % BLOCK
        causal = key_at <= query_at

        def block_body(n, i, k):
            start = blocks + i - (n - 1)
            rel = HALO + i - (n - 1)
            size = n * BLOCK
            keys = kvs[pl.ds(start, n), :, :DH].reshape(size, DH)
            values = kvs[pl.ds(start, n), :, DH:].reshape(size, DH)
            lane = pl.multiple_of(rel * DH, DH)
            keys_t = kts[:, pl.ds(lane, size)]
            values_t = vts[:, pl.ds(lane, size)]
            for pair in range(pairs):
                c0 = pair * 2 * DH
                q2 = jnp.concatenate([qs[i, :, c0 : c0 + DH], qs[i, :, c0 + DH : c0 + 2 * DH]], axis=0)
                g2 = jnp.concatenate([gs[i, :, c0 : c0 + DH], gs[i, :, c0 + DH : c0 + 2 * DH]], axis=0)
                s = lax.dot_general(keys, q2, NT, preferred_element_type=F32)
                diag = jnp.where(causal, s[size - BLOCK :], -jnp.inf)
                s = jnp.concatenate([s[: size - BLOCK], diag], axis=0) if n > 1 else diag
                top = jnp.max(s, axis=0, keepdims=True)
                p = jnp.exp2((s - top) * exponent)
                w = p * (1.0 / jnp.sum(p, axis=0, keepdims=True))
                wb = w.astype(BF16)
                o_t = jnp.dot(values_t, wb, preferred_element_type=F32)
                dp = lax.dot_general(values, g2, NT, preferred_element_type=F32)
                delta = jnp.sum(w * dp, axis=0, keepdims=True)
                ds = (w * (dp - delta)).astype(BF16)
                dq_t = jnp.dot(keys_t, ds, preferred_element_type=F32) * scale
                dk = jnp.dot(ds, q2, preferred_element_type=F32)
                dv = jnp.dot(wb, g2, preferred_element_type=F32)
                acc[pl.ds(rel, n), :, :DH] += dk.reshape(n, BLOCK, DH)
                acc[pl.ds(rel, n), :, DH:] += dv.reshape(n, BLOCK, DH)
                for side in range(2):
                    c1 = c0 + side * DH
                    os[i, :, c1 : c1 + DH] = o_t[:, side * BLOCK : (side + 1) * BLOCK].T.astype(BF16)
                    gqs[k, :, c1 : c1 + DH] = dq_t[:, side * BLOCK : (side + 1) * BLOCK].T.astype(BF16)

        @pl.loop(0, blocks)
        def _(k):
            i = core ^ k
            go_copy(i).wait()
            count = tab[blocks + i]
            at = k if last else ((i // per_src) ^ plane) * per_src + i % per_src
            for n in range(1, DOCMAX + 1):
                @pl.when(count == n)
                def _():
                    block_body(n, i, at)
            out_copy(i).start()

        if last:
            @pl.loop(0, HALO)
            def _(b):
                backs[b, :, :DH] = (acc[b, :, :DH] * scale).astype(BF16)
                backs[b, :, DH:] = acc[b, :, DH:].astype(BF16)

        stores = []

        def store(src, dst):
            copy = pltpu.make_async_copy(src, dst, sem_end.at[slots + len(stores)])
            copy.start()
            stores.append(copy)

        if last:
            store(backs, back_ref)
            store(gqs, gq_ref)
            store(acc.at[pl.ds(HALO, blocks)], main_ref)
        else:
            for k in range(n_src):
                store(gqs.at[pl.ds(k * per_src, per_src)], gq_refs[k])
            store(acc, acc_out)

        for copy in stores:
            copy.wait()

        @pl.loop(0, blocks)
        def _(i):
            out_copy(i).wait()

        for slot in range(slots):
            @pl.when(tab[2 * blocks + 2 + slot] == 0)
            def _():
                pltpu.make_async_copy(zero, slot_ref(slot), sem_end.at[slot]).wait()

    operands = [table, *kv_parts]
    if not first:
        operands += query_parts
    operands.append(grad_slots)
    if not first:
        operands.append(carried)
    out_shape = [jax.ShapeDtypeStruct((*out_form, width), BF16)]
    if last:
        out_shape += [
            jax.ShapeDtypeStruct((blocks, BLOCK, width), BF16),
            jax.ShapeDtypeStruct((blocks, BLOCK, 2 * DH), F32),
            jax.ShapeDtypeStruct((HALO, BLOCK, 2 * DH), BF16),
        ]
    else:
        out_shape += [jax.ShapeDtypeStruct((per_src, BLOCK, width), BF16)] * n_src
        out_shape += [jax.ShapeDtypeStruct((span, BLOCK, 2 * DH), F32)]
    scratch = [
        pltpu.VMEM((blocks, BLOCK, width), BF16),
        pltpu.VMEM((blocks, BLOCK, width), BF16),
        pltpu.VMEM((2 * blocks, BLOCK, 2 * DH), BF16),
        pltpu.VMEM((DH, span * BLOCK), BF16),
        pltpu.VMEM((DH, span * BLOCK), BF16),
        pltpu.VMEM((span, BLOCK, 2 * DH), F32),
        pltpu.VMEM((blocks, BLOCK, width), BF16),
        pltpu.VMEM((blocks, BLOCK, width), BF16),
        pltpu.VMEM((BLOCK, width), BF16),
        pltpu.SemaphoreType.DMA((3 * n_src + 1,)),
        pltpu.SemaphoreType.DMA((blocks,)),
        pltpu.SemaphoreType.DMA((blocks,)),
        pltpu.SemaphoreType.DMA((slots + blocks + 3,)),
    ]
    if last:
        scratch.append(pltpu.VMEM((HALO, BLOCK, 2 * DH), BF16))
    work = blocks * width // DH * 4
    results = pl.pallas_call(
        kernel,
        in_specs=[pl.BlockSpec(memory_space=pltpu.SMEM)] + [ANY] * (len(operands) - 1),
        out_specs=[ANY] * len(out_shape),
        out_shape=out_shape,
        scratch_shapes=scratch,
        cost_estimate=pl.CostEstimate(
            flops=work * 10 * BLOCK**3, bytes_accessed=12 << 20, transcendentals=work * BLOCK**2
        ),
        compiler_params=pltpu.CompilerParams(vmem_limit_bytes=62 << 20),
        name="attend_last" if last else "attend_first",
    )(*operands)
    return results


def finish(core_index, rows, main, back):
    blocks, _, width = rows.shape
    base = blocks - HALO
    scale = 1.0 / math.sqrt(DH)

    def kernel(core_ref, rows_ref, main_ref, back_ref, *refs):
        outs, (held, mains, backs, sem_in, sem_out) = refs[:blocks], refs[blocks:]
        core = core_ref[0]
        loads = [
            pltpu.make_async_copy(main_ref, mains, sem_in.at[0]),
            pltpu.make_async_copy(back_ref, backs, sem_in.at[1]),
            pltpu.make_async_copy(rows_ref, held.at[:, :, :width], sem_in.at[2]),
        ]
        for copy in loads:
            copy.start()
        for copy in loads:
            copy.wait()
        stores = []
        for k in range(blocks):
            i = core ^ k
            near = jnp.where(i >= base, 1.0, 0.0)
            term = backs[jnp.maximum(i - base, 0)].astype(F32) * near
            held[k, :, width : width + DH] = (mains[i, :, :DH] * scale + term[:, :DH]).astype(BF16)
            held[k, :, width + DH :] = (mains[i, :, DH:] + term[:, DH:]).astype(BF16)
            copy = pltpu.make_async_copy(held.at[k], outs[k], sem_out.at[k])
            copy.start()
            stores.append(copy)
        for copy in stores:
            copy.wait()

    total = width + 2 * DH
    return pl.pallas_call(
        kernel,
        in_specs=[pl.BlockSpec(memory_space=pltpu.SMEM)] + [ANY] * 3,
        out_specs=[ANY] * blocks,
        out_shape=[jax.ShapeDtypeStruct((BLOCK, total), BF16)] * blocks,
        scratch_shapes=[
            pltpu.VMEM((blocks, BLOCK, total), BF16),
            pltpu.VMEM((blocks, BLOCK, 2 * DH), F32),
            pltpu.VMEM((HALO, BLOCK, 2 * DH), BF16),
            pltpu.SemaphoreType.DMA((3,)),
            pltpu.SemaphoreType.DMA((blocks,)),
        ],
        cost_estimate=pl.CostEstimate(flops=0, bytes_accessed=5 << 20, transcendentals=0),
        compiler_params=pltpu.CompilerParams(vmem_limit_bytes=62 << 20),
        name="finish",
    )(core_index, rows, main, back)


def place_rows(block_index, arrived, last_rows, groups):
    repeats = groups // KVH
    width = QH // groups * DH
    half = width // CHUNKS
    first_row = arrived.shape[1] - BLOCK

    def kernel(*refs):
        at_ref, arrived_ref, *refs = refs
        lasts, refs = refs[:groups], refs[groups:]
        gq_ref, gk_ref, gv_ref, rows, held, sums, sem_in, sem_out = refs
        at = at_ref[0]
        loads, stores = [], []

        def load(src, dst):
            copy = pltpu.make_async_copy(src, dst, sem_in.at[len(loads)])
            copy.start()
            loads.append(copy)

        def store(src, dst):
            copy = pltpu.make_async_copy(src, dst, sem_out.at[len(stores)])
            copy.start()
            stores.append(copy)

        for r in range(groups):
            load(arrived_ref.at[r, first_row:, :], rows.at[:, r * width : r * width + half])
        for k in range(groups):
            group = at ^ k
            col = pl.multiple_of(group * width + half, half)
            load(lasts[k].at[:, :half], rows.at[:, pl.ds(col, half)])
            load(lasts[k].at[:, half:], held.at[group])
        for copy in loads:
            copy.wait()
        store(rows, gq_ref)
        for head in range(KVH):
            total = held[head * repeats].astype(F32)
            for extra in range(1, repeats):
                total += held[head * repeats + extra].astype(F32)
            sums[0, :, head * DH : (head + 1) * DH] = total[:, :DH].astype(BF16)
            sums[1, :, head * DH : (head + 1) * DH] = total[:, DH:].astype(BF16)
        store(sums.at[0], gk_ref)
        store(sums.at[1], gv_ref)
        for copy in stores:
            copy.wait()

    return pl.pallas_call(
        kernel,
        in_specs=[pl.BlockSpec(memory_space=pltpu.SMEM)] + [ANY] * (groups + 1),
        out_specs=[ANY] * 3,
        out_shape=[
            jax.ShapeDtypeStruct((BLOCK, QH * DH), BF16),
            jax.ShapeDtypeStruct((BLOCK, KVH * DH), BF16),
            jax.ShapeDtypeStruct((BLOCK, KVH * DH), BF16),
        ],
        scratch_shapes=[
            pltpu.VMEM((BLOCK, QH * DH), BF16),
            pltpu.VMEM((groups, BLOCK, 2 * DH), BF16),
            pltpu.VMEM((2, BLOCK, KVH * DH), BF16),
            pltpu.SemaphoreType.DMA((3 * groups,)),
            pltpu.SemaphoreType.DMA((3,)),
        ],
        cost_estimate=pl.CostEstimate(flops=0, bytes_accessed=6 << 20, transcendentals=0),
        compiler_params=pltpu.CompilerParams(vmem_limit_bytes=62 << 20),
        name="place_rows",
    )(block_index, arrived, *last_rows)


def place_out(parts, rows, chunk, held):
    groups, _, half = parts.shape

    def kernel(*refs):
        in_ref, (out_ref, buf, sem_in, sem_out) = refs[0], refs[-4:]
        loads = [
            pltpu.make_async_copy(in_ref.at[r, :rows, :], buf.at[r], sem_in.at[r])
            for r in range(groups)
        ]
        stores = []
        for copy in loads:
            copy.start()
        for r in range(groups):
            col = (r * CHUNKS + chunk) * half
            loads[r].wait()
            copy = pltpu.make_async_copy(buf.at[r], out_ref.at[:, col : col + half], sem_out.at[r])
            copy.start()
            stores.append(copy)
        for copy in stores:
            copy.wait()

    operands = [parts] if held is None else [parts, held]
    return pl.pallas_call(
        kernel,
        in_specs=[ANY] * len(operands),
        out_specs=ANY,
        out_shape=jax.ShapeDtypeStruct((rows, QH * DH), BF16),
        scratch_shapes=[
            pltpu.VMEM((groups, rows, half), BF16),
            pltpu.SemaphoreType.DMA((groups,)),
            pltpu.SemaphoreType.DMA((groups,)),
        ],
        input_output_aliases={} if held is None else {1: 0},
        cost_estimate=pl.CostEstimate(
            flops=0, bytes_accessed=4 * groups * rows * half, transcendentals=0
        ),
        compiler_params=pltpu.CompilerParams(vmem_limit_bytes=62 << 20),
        name="place_out",
    )(*operands)


def body(shape, query_rows, key_rows, value_rows, grad_out, doc_ids, route_table):
    n_seq, n_plane, per_plane = shape
    groups = n_seq * per_plane
    blocks = n_plane * per_plane
    slots = route_table.shape[1] * route_table.shape[2]
    axes = ("seq", "hs", "hp")
    plane_axes = ("seq", "hp")
    seq_at = lax.axis_index("seq")
    plane = lax.axis_index("hs")
    part = lax.axis_index("hp")
    core = seq_at * per_plane + part

    def device(seq, hs, hp):
        return (seq * n_plane + hs) * per_plane + hp

    every = [(a, b, c) for a in range(n_seq) for b in range(n_plane) for c in range(per_plane)]

    def swap(x):
        return lax.all_to_all(x, plane_axes, split_axis=0, concat_axis=0, tiled=True)

    def along(x, k):
        return lax.ppermute(x, axes, [(device(a, b, c), device(a, b ^ k, c)) for a, b, c in every])

    def home(x, k):
        pairs = []
        for a, b, c in every:
            index = (a * per_plane + c) ^ k
            pairs.append((device(a, b, c), device(b, index // per_plane, index % per_plane)))
        return lax.ppermute(x, axes, pairs)

    routes = lax.dynamic_index_in_dim(route_table, plane, 0, keepdims=False).reshape(slots)
    match = routes[None, :] == jnp.arange(blocks, dtype=jnp.int32)[:, None]
    slot_of = jnp.sum(jnp.where(match, jnp.arange(slots, dtype=jnp.int32)[None, :], 0), axis=1)
    docs_pad = jnp.concatenate([jnp.full((HALO,), -1, jnp.int32), doc_ids])
    docs = lax.dynamic_slice_in_dim(docs_pad, plane * blocks, blocks + HALO, 0)
    own = docs[HALO:]
    counts = sum(
        (docs[HALO - d : HALO - d + blocks] == own).astype(jnp.int32) for d in range(DOCMAX)
    )
    live = (routes < blocks).astype(jnp.int32)
    table = jnp.concatenate(
        [slot_of, counts, jnp.stack([plane, core]).astype(jnp.int32), live]
    )

    def spread(x):
        return x.reshape((n_seq, per_plane) + x.shape[1:])

    def by_slot(x):
        return x.reshape(slots, BLOCK, x.shape[-1])

    first_pack = pack_first(query_rows, key_rows, value_rows, groups)
    first_plane = spread(swap(first_pack))
    grad_pack = pack_half(grad_out, 0, groups)
    grad_pack_second = pack_half(grad_out, 1, groups)
    width = grad_pack.shape[-1]

    plane_index = plane.astype(jnp.int32).reshape(1)
    kv_parts, query_parts = relay_in(plane_index, first_plane, width)
    for k in range(1, n_plane):
        kv_parts[k] = along(kv_parts[k], k)
    for k in range(1, n_plane):
        query_parts[k] = along(query_parts[k], k)
    grad_first = by_slot(swap(grad_pack))
    grad_second = by_slot(swap(grad_pack_second))

    rows = grad_out.shape[0]
    out_first, *rows_first, carried = attend(
        table, kv_parts, None, grad_first, None, False, blocks, (groups, rows)
    )
    for k in range(1, n_plane):
        rows_first[k] = along(rows_first[k], k)
    back_first = swap(out_first)
    out_second, rows_second, main, back = attend(
        table, kv_parts, query_parts, grad_second, carried, True, blocks, (groups, rows + BLOCK)
    )
    down = [(device(a, b, c), device(a, b - 1, c)) for a, b, c in every if b]
    back = lax.ppermute(back, axes, down)
    out_second = relay_out(plane_index, rows_first, out_second)
    back_second = swap(out_second)
    rows_second = finish(core.astype(jnp.int32).reshape(1), rows_second, main, back)
    home_second = []
    for k in range(blocks):
        home_second.append(home(rows_second[k], k))

    attn_out = place_out(back_first, rows, 0, None)
    block_index = (plane * per_plane + part).astype(jnp.int32).reshape(1)
    grad_query, grad_key, grad_value = place_rows(
        block_index, back_second, home_second, groups
    )
    attn_out = place_out(back_second, rows, 1, attn_out)
    return (attn_out, grad_query, grad_key, grad_value)


def whole(shape, *args):
    return body(shape, *args)


def solution(mesh):
    n_seq, n_head = mesh.shape["seq"], mesh.shape["head"]
    per_plane = n_head // n_seq
    shape = (n_seq, n_seq, per_plane)
    wide = Mesh(mesh.devices.reshape(shape), ("seq", "hs", "hp"))
    rows = P(("seq", "hs", "hp"), None)
    return jax.shard_map(
        functools.partial(whole, shape),
        mesh=wide,
        in_specs=(rows, rows, rows, rows, P(), P()),
        out_specs=(rows, rows, rows, rows),
        check_vma=False,
    )
```

```python
import functools
import math

import jax
import jax.numpy as jnp
from jax import lax
from jax.experimental import pallas as pl
from jax.experimental.pallas import tpu as pltpu
from jax.sharding import Mesh
from jax.sharding import PartitionSpec as P


QH = 64
KVH = 8
DH = 128
BLOCK = 128
DOCMAX = 7
HALO = DOCMAX - 1
CHUNKS = 2

ANY = pl.BlockSpec(memory_space=pl.ANY)
NT = (((1,), (1,)), ((), ()))
F32 = jnp.float32
BF16 = jnp.bfloat16


def pack(sources, groups):
    count = sources[0][0].shape[0]
    total = sum(width for _, width, _ in sources)

    def kernel(*refs):
        ins, out_ref, held, sem_in, sem_out = refs[: len(sources)], *refs[len(sources) :]
        loads, stores = [], []
        for r in range(groups):
            at = 0
            for n, (_, width, index) in enumerate(sources):
                col = index(r) * width
                copy = pltpu.make_async_copy(
                    ins[n].at[:, col : col + width],
                    held.at[r, :, at : at + width],
                    sem_in.at[r * len(sources) + n],
                )
                copy.start()
                loads.append(copy)
                at += width
        for r in range(groups):
            for n in range(len(sources)):
                loads[r * len(sources) + n].wait()
            copy = pltpu.make_async_copy(held.at[r], out_ref.at[r], sem_out.at[r])
            copy.start()
            stores.append(copy)
        for copy in stores:
            copy.wait()

    return pl.pallas_call(
        kernel,
        in_specs=[ANY] * len(sources),
        out_specs=ANY,
        out_shape=jax.ShapeDtypeStruct((groups, count, total), BF16),
        scratch_shapes=[
            pltpu.VMEM((groups, count, total), BF16),
            pltpu.SemaphoreType.DMA((groups * len(sources),)),
            pltpu.SemaphoreType.DMA((groups,)),
        ],
        cost_estimate=pl.CostEstimate(
            flops=0, bytes_accessed=4 * groups * count * total, transcendentals=0
        ),
        compiler_params=pltpu.CompilerParams(vmem_limit_bytes=62 << 20),
    )(*[rows for rows, _, _ in sources])


def pack_first(query_rows, key_rows, value_rows, groups):
    half = QH // groups * DH // CHUNKS
    repeats = groups // KVH
    sources = [
        (query_rows, half, lambda r: r * CHUNKS),
        (key_rows, DH, lambda r: r // repeats),
        (value_rows, DH, lambda r: r // repeats),
    ]
    return pack(sources, groups)


def pack_half(rows, chunk, groups):
    half = QH // groups * DH // CHUNKS
    return pack([(rows, half, lambda r: r * CHUNKS + chunk)], groups)


def pack_grad(core_index, rows, chunk, groups):
    count = rows.shape[0]
    half = QH // groups * DH // CHUNKS

    def kernel(core_ref, in_ref, *refs):
        outs, (held, sem_in, sem_out) = refs[:groups], refs[groups:]
        loads, stores = [], []
        for k in range(groups):
            col = pl.multiple_of(((core_ref[0] ^ k) * CHUNKS + chunk) * half, half)
            copy = pltpu.make_async_copy(in_ref.at[:, pl.ds(col, half)], held.at[k], sem_in.at[k])
            copy.start()
            loads.append(copy)
        for k in range(groups):
            loads[k].wait()
            copy = pltpu.make_async_copy(held.at[k], outs[k], sem_out.at[k])
            copy.start()
            stores.append(copy)
        for copy in stores:
            copy.wait()

    return list(
        pl.pallas_call(
            kernel,
            in_specs=[pl.BlockSpec(memory_space=pltpu.SMEM), ANY],
            out_specs=[ANY] * groups,
            out_shape=[jax.ShapeDtypeStruct((count, half), BF16)] * groups,
            scratch_shapes=[
                pltpu.VMEM((groups, count, half), BF16),
                pltpu.SemaphoreType.DMA((groups,)),
                pltpu.SemaphoreType.DMA((groups,)),
            ],
            cost_estimate=pl.CostEstimate(
                flops=0, bytes_accessed=4 * groups * count * half, transcendentals=0
            ),
            compiler_params=pltpu.CompilerParams(vmem_limit_bytes=62 << 20),
            name="pack_grad",
        )(core_index, rows)
    )


def relay_in(plane_index, arrived, width):
    n_plane, per_plane, _, total = arrived.shape
    halo = total - width
    form = (per_plane, BLOCK, total + halo)
    copies = 2 if halo else 1

    def kernel(plane_ref, in_ref, *refs):
        outs, (held, sem_in, sem_out) = refs[:n_plane], refs[n_plane:]
        loads, stores = [], []
        for k in range(n_plane):
            to = plane_ref[0] ^ k
            views = [(in_ref.at[to], held.at[k, :, :, :total] if halo else held.at[k])]
            if halo:
                near = jnp.maximum(to - 1, 0)
                views.append((in_ref.at[near, :, :, width:], held.at[k, :, :, total:]))
            for n, (src, dst) in enumerate(views):
                copy = pltpu.make_async_copy(src, dst, sem_in.at[copies * k + n])
                copy.start()
                loads.append(copy)
        for k in range(n_plane):
            for copy in loads[copies * k : copies * (k + 1)]:
                copy.wait()
            copy = pltpu.make_async_copy(held.at[k], outs[k], sem_out.at[k])
            copy.start()
            stores.append(copy)
        for copy in stores:
            copy.wait()

    return list(
        pl.pallas_call(
            kernel,
            in_specs=[pl.BlockSpec(memory_space=pltpu.SMEM), ANY],
            out_specs=[ANY] * n_plane,
            out_shape=[jax.ShapeDtypeStruct(form, BF16)] * n_plane,
            scratch_shapes=[
                pltpu.VMEM((n_plane, *form), BF16),
                pltpu.SemaphoreType.DMA((copies * n_plane,)),
                pltpu.SemaphoreType.DMA((n_plane,)),
            ],
            cost_estimate=pl.CostEstimate(flops=0, bytes_accessed=4 << 20, transcendentals=0),
            compiler_params=pltpu.CompilerParams(vmem_limit_bytes=62 << 20),
            name="relay_in",
        )(plane_index, arrived)
    )


def relay_out(plane_index, parts, held):
    n_plane = len(parts)
    per_plane, _, width = parts[0].shape
    first_row = held.shape[1] - BLOCK

    def kernel(plane_ref, *refs):
        ins, (_, out_ref, buf, sem_in, sem_out) = refs[:n_plane], refs[n_plane:]
        loads, stores = [], []
        for k in range(n_plane):
            copy = pltpu.make_async_copy(ins[k], buf.at[k], sem_in.at[k])
            copy.start()
            loads.append(copy)
        for k in range(n_plane):
            loads[k].wait()
            at = (plane_ref[0] ^ k) * per_plane
            copy = pltpu.make_async_copy(
                buf.at[k], out_ref.at[pl.ds(at, per_plane), first_row:, :], sem_out.at[k]
            )
            copy.start()
            stores.append(copy)
        for copy in stores:
            copy.wait()

    return pl.pallas_call(
        kernel,
        in_specs=[pl.BlockSpec(memory_space=pltpu.SMEM)] + [ANY] * (n_plane + 1),
        out_specs=ANY,
        out_shape=jax.ShapeDtypeStruct(held.shape, BF16),
        scratch_shapes=[
            pltpu.VMEM((n_plane, per_plane, BLOCK, width), BF16),
            pltpu.SemaphoreType.DMA((n_plane,)),
            pltpu.SemaphoreType.DMA((n_plane,)),
        ],
        input_output_aliases={n_plane + 1: 0},
        cost_estimate=pl.CostEstimate(flops=0, bytes_accessed=2 << 20, transcendentals=0),
        compiler_params=pltpu.CompilerParams(vmem_limit_bytes=62 << 20),
        name="relay_out",
    )(plane_index, *parts, held)


def attend(table, kv_parts, query_parts, grad_parts, carried, last, shard_blocks, out_form):
    n_src = len(kv_parts)
    per_src = kv_parts[0].shape[0]
    blocks = shard_blocks
    width = grad_parts[0].shape[-1]
    per_core = grad_parts[0].shape[0] // BLOCK
    slots = per_core * len(grad_parts)
    owner = 2 * blocks + 2
    base = blocks - HALO
    span = blocks + HALO
    scale = 1.0 / math.sqrt(DH)
    exponent = scale * math.log2(math.e)
    first = carried is None

    def kernel(*refs):
        refs = list(refs)
        tab = refs.pop(0)
        kv_refs = [refs.pop(0) for _ in range(n_src)]
        q_refs = kv_refs if first else [refs.pop(0) for _ in range(n_src)]
        go_refs = [refs.pop(0) for _ in grad_parts]
        carried_ref = None if first else refs.pop(0)
        out_ref = refs.pop(0)
        if last:
            gq_ref, main_ref, back_ref = refs.pop(0), refs.pop(0), refs.pop(0)
        else:
            gq_refs = [refs.pop(0) for _ in range(n_src)]
            acc_out = refs.pop(0)
        qs, gs, kvs, kts, vts, acc, os, gqs, zero, sem_in, sem_go, sem_out, sem_end = refs[:13]
        if last:
            backs = refs[13]
        plane = tab[2 * blocks]
        core = tab[2 * blocks + 1]

        loads = []

        def load(src, dst):
            copy = pltpu.make_async_copy(src, dst, sem_in.at[len(loads)])
            copy.start()
            loads.append(copy)

        for k in range(n_src):
            at = (plane ^ k) * per_src
            load(kv_refs[k].at[:, :, width : width + 2 * DH], kvs.at[pl.ds(blocks + at, per_src)])
            load(kv_refs[k].at[:, :, width + 2 * DH :], kvs.at[pl.ds(at, per_src)])
            load(q_refs[k].at[:, :, :width], qs.at[pl.ds(at, per_src)])
        if not first:
            load(carried_ref, acc)

        def slot_ref(slot):
            row = pl.multiple_of(slot % per_core * BLOCK, BLOCK)
            return out_ref.at[slot // per_core, pl.ds(row, BLOCK), :]

        def go_copy(k, at, i):
            rows = go_refs[k].at[at * BLOCK : (at + 1) * BLOCK, :]
            return pltpu.make_async_copy(rows, gs.at[i], sem_go.at[i])

        def out_copy(i):
            return pltpu.make_async_copy(os.at[i], slot_ref(tab[i]), sem_out.at[i])

        for k in range(len(grad_parts)):
            for at in range(per_core):
                i = tab[owner + (core ^ k) * per_core + at]

                @pl.when(i < blocks)
                def _():
                    go_copy(k, at, i).start()

        zero[...] = jnp.zeros_like(zero)
        for slot in range(slots):
            @pl.when(tab[owner + slot] >= blocks)
            def _():
                pltpu.make_async_copy(zero, slot_ref(slot), sem_end.at[slot]).start()

        if first:
            acc[...] = jnp.zeros_like(acc)
        for copy in loads:
            copy.wait()

        @pl.loop(0, span)
        def _(b):
            at = pl.multiple_of(b * DH, DH)
            kts[:, pl.ds(at, DH)] = kvs[base + b, :, :DH].T
            vts[:, pl.ds(at, DH)] = kvs[base + b, :, DH:].T

        key_at = lax.broadcasted_iota(jnp.int32, (BLOCK, width), 0)
        query_at = lax.broadcasted_iota(jnp.int32, (BLOCK, width), 1) % BLOCK
        causal = key_at <= query_at

        def block_body(n, i, k):
            start = blocks + i - (n - 1)
            rel = HALO + i - (n - 1)
            size = n * BLOCK
            keys = kvs[pl.ds(start, n), :, :DH].reshape(size, DH)
            values = kvs[pl.ds(start, n), :, DH:].reshape(size, DH)
            lane = pl.multiple_of(rel * DH, DH)
            keys_t = kts[:, pl.ds(lane, size)]
            values_t = vts[:, pl.ds(lane, size)]
            cols = [slice(c, c + DH) for c in range(0, width, DH)]
            q_all = jnp.concatenate([qs[i, :, c] for c in cols], axis=0)
            g_all = jnp.concatenate([gs[i, :, c] for c in cols], axis=0)
            s = lax.dot_general(keys, q_all, NT, preferred_element_type=F32)
            dp = lax.dot_general(values, g_all, NT, preferred_element_type=F32)
            diag = jnp.where(causal, s[size - BLOCK :], -jnp.inf)
            s = jnp.concatenate([s[: size - BLOCK], diag], axis=0) if n > 1 else diag
            top = jnp.max(s, axis=0, keepdims=True)
            p = jnp.exp2((s - top) * exponent)
            w = p * (1.0 / jnp.sum(p, axis=0, keepdims=True))
            wb = w.astype(BF16)
            delta = jnp.sum(w * dp, axis=0, keepdims=True)
            ds = (w * (dp - delta)).astype(BF16)
            o_t = jnp.dot(values_t, wb, preferred_element_type=F32)
            dq_t = jnp.dot(keys_t, ds, preferred_element_type=F32) * scale
            dk = jnp.dot(ds, q_all, preferred_element_type=F32)
            dv = jnp.dot(wb, g_all, preferred_element_type=F32)
            acc[pl.ds(rel, n), :, :DH] += dk.reshape(n, BLOCK, DH)
            acc[pl.ds(rel, n), :, DH:] += dv.reshape(n, BLOCK, DH)
            for c in cols:
                os[i, :, c] = o_t[:, c].T.astype(BF16)
                gqs[k, :, c] = dq_t[:, c].T.astype(BF16)

        @pl.loop(0, blocks)
        def _(k):
            i = core ^ k
            go_copy(0, 0, i).wait()
            count = tab[blocks + i]
            at = k if last else ((i // per_src) ^ plane) * per_src + i % per_src
            for n in range(1, DOCMAX + 1):
                @pl.when(count == n)
                def _():
                    block_body(n, i, at)
            out_copy(i).start()

        if last:
            @pl.loop(0, HALO)
            def _(b):
                backs[b, :, :DH] = (acc[b, :, :DH] * scale).astype(BF16)
                backs[b, :, DH:] = acc[b, :, DH:].astype(BF16)

        stores = []

        def store(src, dst):
            copy = pltpu.make_async_copy(src, dst, sem_end.at[slots + len(stores)])
            copy.start()
            stores.append(copy)

        if last:
            store(backs, back_ref)
            store(gqs, gq_ref)
            store(acc.at[pl.ds(HALO, blocks)], main_ref)
        else:
            for k in range(n_src):
                store(gqs.at[pl.ds(k * per_src, per_src)], gq_refs[k])
            store(acc, acc_out)

        for copy in stores:
            copy.wait()

        @pl.loop(0, blocks)
        def _(i):
            out_copy(i).wait()

        for slot in range(slots):
            @pl.when(tab[owner + slot] >= blocks)
            def _():
                pltpu.make_async_copy(zero, slot_ref(slot), sem_end.at[slot]).wait()

    operands = [table, *kv_parts]
    if not first:
        operands += query_parts
    operands += grad_parts
    if not first:
        operands.append(carried)
    out_shape = [jax.ShapeDtypeStruct((*out_form, width), BF16)]
    if last:
        out_shape += [
            jax.ShapeDtypeStruct((blocks, BLOCK, width), BF16),
            jax.ShapeDtypeStruct((blocks, BLOCK, 2 * DH), F32),
            jax.ShapeDtypeStruct((HALO, BLOCK, 2 * DH), BF16),
        ]
    else:
        out_shape += [jax.ShapeDtypeStruct((per_src, BLOCK, width), BF16)] * n_src
        out_shape += [jax.ShapeDtypeStruct((span, BLOCK, 2 * DH), F32)]
    scratch = [
        pltpu.VMEM((blocks, BLOCK, width), BF16),
        pltpu.VMEM((blocks, BLOCK, width), BF16),
        pltpu.VMEM((2 * blocks, BLOCK, 2 * DH), BF16),
        pltpu.VMEM((DH, span * BLOCK), BF16),
        pltpu.VMEM((DH, span * BLOCK), BF16),
        pltpu.VMEM((span, BLOCK, 2 * DH), F32),
        pltpu.VMEM((blocks, BLOCK, width), BF16),
        pltpu.VMEM((blocks, BLOCK, width), BF16),
        pltpu.VMEM((BLOCK, width), BF16),
        pltpu.SemaphoreType.DMA((3 * n_src + 1,)),
        pltpu.SemaphoreType.DMA((blocks,)),
        pltpu.SemaphoreType.DMA((blocks,)),
        pltpu.SemaphoreType.DMA((slots + blocks + 3,)),
    ]
    if last:
        scratch.append(pltpu.VMEM((HALO, BLOCK, 2 * DH), BF16))
    work = blocks * width // DH * 4
    results = pl.pallas_call(
        kernel,
        in_specs=[pl.BlockSpec(memory_space=pltpu.SMEM)] + [ANY] * (len(operands) - 1),
        out_specs=[ANY] * len(out_shape),
        out_shape=out_shape,
        scratch_shapes=scratch,
        cost_estimate=pl.CostEstimate(
            flops=work * 10 * BLOCK**3, bytes_accessed=12 << 20, transcendentals=work * BLOCK**2
        ),
        compiler_params=pltpu.CompilerParams(vmem_limit_bytes=62 << 20),
        name="attend_last" if last else "attend_first",
    )(*operands)
    return results


def finish(core_index, rows, main, back):
    blocks, _, width = rows.shape
    base = blocks - HALO
    scale = 1.0 / math.sqrt(DH)

    def kernel(core_ref, rows_ref, main_ref, back_ref, *refs):
        outs, (held, mains, backs, sem_in, sem_out) = refs[:blocks], refs[blocks:]
        core = core_ref[0]
        loads = [
            pltpu.make_async_copy(main_ref, mains, sem_in.at[0]),
            pltpu.make_async_copy(back_ref, backs, sem_in.at[1]),
            pltpu.make_async_copy(rows_ref, held.at[:, :, :width], sem_in.at[2]),
        ]
        for copy in loads:
            copy.start()
        for copy in loads:
            copy.wait()
        stores = []
        for k in range(blocks):
            i = core ^ k
            near = jnp.where(i >= base, 1.0, 0.0)
            term = backs[jnp.maximum(i - base, 0)].astype(F32) * near
            held[k, :, width : width + DH] = (mains[i, :, :DH] * scale + term[:, :DH]).astype(BF16)
            held[k, :, width + DH :] = (mains[i, :, DH:] + term[:, DH:]).astype(BF16)
            copy = pltpu.make_async_copy(held.at[k], outs[k], sem_out.at[k])
            copy.start()
            stores.append(copy)
        for copy in stores:
            copy.wait()

    total = width + 2 * DH
    return pl.pallas_call(
        kernel,
        in_specs=[pl.BlockSpec(memory_space=pltpu.SMEM)] + [ANY] * 3,
        out_specs=[ANY] * blocks,
        out_shape=[jax.ShapeDtypeStruct((BLOCK, total), BF16)] * blocks,
        scratch_shapes=[
            pltpu.VMEM((blocks, BLOCK, total), BF16),
            pltpu.VMEM((blocks, BLOCK, 2 * DH), F32),
            pltpu.VMEM((HALO, BLOCK, 2 * DH), BF16),
            pltpu.SemaphoreType.DMA((3,)),
            pltpu.SemaphoreType.DMA((blocks,)),
        ],
        cost_estimate=pl.CostEstimate(flops=0, bytes_accessed=5 << 20, transcendentals=0),
        compiler_params=pltpu.CompilerParams(vmem_limit_bytes=62 << 20),
        name="finish",
    )(core_index, rows, main, back)


def place_rows(block_index, last_rows, groups):
    repeats = groups // KVH
    width = QH // groups * DH
    half = width // CHUNKS

    def kernel(*refs):
        at_ref, *refs = refs
        lasts, refs = refs[:groups], refs[groups:]
        gq_ref, gk_ref, gv_ref, rows, held, sums, sem_in, sem_out = refs
        at = at_ref[0]
        loads, stores = [], []

        def load(src, dst):
            copy = pltpu.make_async_copy(src, dst, sem_in.at[len(loads)])
            copy.start()
            loads.append(copy)

        def store(src, dst):
            copy = pltpu.make_async_copy(src, dst, sem_out.at[len(stores)])
            copy.start()
            stores.append(copy)

        for k in range(groups):
            load(lasts[k].at[:, :half], rows.at[k])
            load(lasts[k].at[:, half:], held.at[at ^ k])
        for k in range(groups):
            col = pl.multiple_of((at ^ k) * width + half, half)
            loads[2 * k].wait()
            store(rows.at[k], gq_ref.at[:, pl.ds(col, half)])
        for k in range(groups):
            loads[2 * k + 1].wait()
        for head in range(KVH):
            total = held[head * repeats].astype(F32)
            for extra in range(1, repeats):
                total += held[head * repeats + extra].astype(F32)
            sums[0, :, head * DH : (head + 1) * DH] = total[:, :DH].astype(BF16)
            sums[1, :, head * DH : (head + 1) * DH] = total[:, DH:].astype(BF16)
        store(sums.at[0], gk_ref)
        store(sums.at[1], gv_ref)
        for copy in stores:
            copy.wait()

    return pl.pallas_call(
        kernel,
        in_specs=[pl.BlockSpec(memory_space=pltpu.SMEM)] + [ANY] * groups,
        out_specs=[ANY] * 3,
        out_shape=[
            jax.ShapeDtypeStruct((BLOCK, QH * DH), BF16),
            jax.ShapeDtypeStruct((BLOCK, KVH * DH), BF16),
            jax.ShapeDtypeStruct((BLOCK, KVH * DH), BF16),
        ],
        scratch_shapes=[
            pltpu.VMEM((groups, BLOCK, half), BF16),
            pltpu.VMEM((groups, BLOCK, 2 * DH), BF16),
            pltpu.VMEM((2, BLOCK, KVH * DH), BF16),
            pltpu.SemaphoreType.DMA((2 * groups,)),
            pltpu.SemaphoreType.DMA((groups + 2,)),
        ],
        cost_estimate=pl.CostEstimate(flops=0, bytes_accessed=4 << 20, transcendentals=0),
        compiler_params=pltpu.CompilerParams(vmem_limit_bytes=62 << 20),
        name="place_rows",
    )(block_index, *last_rows)


def place_last(parts, out, grad_query):
    groups, total, half = parts.shape
    rows = total - BLOCK

    def kernel(in_ref, _, __, out_ref, gq_ref, buf, sem_in, sem_out):
        loads = [pltpu.make_async_copy(in_ref.at[r], buf.at[r], sem_in.at[r]) for r in range(groups)]
        stores = []
        for copy in loads:
            copy.start()
        for r in range(groups):
            first, second = 2 * r * half, (2 * r + 1) * half
            loads[r].wait()
            pairs = [
                (buf.at[r, :rows, :], out_ref.at[:, second : second + half]),
                (buf.at[r, rows:, :], gq_ref.at[:, first : first + half]),
            ]
            for n, (src, dst) in enumerate(pairs):
                copy = pltpu.make_async_copy(src, dst, sem_out.at[2 * r + n])
                copy.start()
                stores.append(copy)
        for copy in stores:
            copy.wait()

    return pl.pallas_call(
        kernel,
        in_specs=[ANY] * 3,
        out_specs=[ANY] * 2,
        out_shape=[
            jax.ShapeDtypeStruct(out.shape, BF16),
            jax.ShapeDtypeStruct(grad_query.shape, BF16),
        ],
        scratch_shapes=[
            pltpu.VMEM((groups, total, half), BF16),
            pltpu.SemaphoreType.DMA((groups,)),
            pltpu.SemaphoreType.DMA((2 * groups,)),
        ],
        input_output_aliases={1: 0, 2: 1},
        cost_estimate=pl.CostEstimate(flops=0, bytes_accessed=6 << 20, transcendentals=0),
        compiler_params=pltpu.CompilerParams(vmem_limit_bytes=62 << 20),
        name="place_last",
    )(parts, out, grad_query)


def place_out(parts):
    groups, rows, half = parts.shape

    def kernel(in_ref, out_ref, buf, sem_in, sem_out):
        loads = [pltpu.make_async_copy(in_ref.at[r], buf.at[r], sem_in.at[r]) for r in range(groups)]
        stores = []
        for copy in loads:
            copy.start()
        for r in range(groups):
            col = CHUNKS * r * half
            loads[r].wait()
            copy = pltpu.make_async_copy(buf.at[r], out_ref.at[:, col : col + half], sem_out.at[r])
            copy.start()
            stores.append(copy)
        for copy in stores:
            copy.wait()

    return pl.pallas_call(
        kernel,
        in_specs=[ANY],
        out_specs=ANY,
        out_shape=jax.ShapeDtypeStruct((rows, QH * DH), BF16),
        scratch_shapes=[
            pltpu.VMEM((groups, rows, half), BF16),
            pltpu.SemaphoreType.DMA((groups,)),
            pltpu.SemaphoreType.DMA((groups,)),
        ],
        cost_estimate=pl.CostEstimate(
            flops=0, bytes_accessed=4 * groups * rows * half, transcendentals=0
        ),
        compiler_params=pltpu.CompilerParams(vmem_limit_bytes=62 << 20),
        name="place_out",
    )(parts)


def body(shape, query_rows, key_rows, value_rows, grad_out, doc_ids, route_table):
    n_seq, n_plane, per_plane = shape
    groups = n_seq * per_plane
    blocks = n_plane * per_plane
    slots = route_table.shape[1] * route_table.shape[2]
    axes = ("seq", "hs", "hp")
    plane_axes = ("seq", "hp")
    seq_at = lax.axis_index("seq")
    plane = lax.axis_index("hs")
    part = lax.axis_index("hp")
    core = seq_at * per_plane + part

    def device(seq, hs, hp):
        return (seq * n_plane + hs) * per_plane + hp

    every = [(a, b, c) for a in range(n_seq) for b in range(n_plane) for c in range(per_plane)]

    def swap(x):
        return lax.all_to_all(x, plane_axes, split_axis=0, concat_axis=0, tiled=True)

    def along(x, k):
        return lax.ppermute(x, axes, [(device(a, b, c), device(a, b ^ k, c)) for a, b, c in every])

    def home(x, k):
        pairs = []
        for a, b, c in every:
            index = (a * per_plane + c) ^ k
            pairs.append((device(a, b, c), device(b, index // per_plane, index % per_plane)))
        return lax.ppermute(x, axes, pairs)

    routes = lax.dynamic_index_in_dim(route_table, plane, 0, keepdims=False).reshape(slots)
    match = routes[None, :] == jnp.arange(blocks, dtype=jnp.int32)[:, None]
    slot_of = jnp.sum(jnp.where(match, jnp.arange(slots, dtype=jnp.int32)[None, :], 0), axis=1)
    docs_pad = jnp.concatenate([jnp.full((HALO,), -1, jnp.int32), doc_ids])
    docs = lax.dynamic_slice_in_dim(docs_pad, plane * blocks, blocks + HALO, 0)
    own = docs[HALO:]
    counts = sum(
        (docs[HALO - d : HALO - d + blocks] == own).astype(jnp.int32) for d in range(DOCMAX)
    )
    table = jnp.concatenate([slot_of, counts, jnp.stack([plane, core]).astype(jnp.int32), routes])

    def spread(x):
        return x.reshape((n_seq, per_plane) + x.shape[1:])

    def across(x, k):
        pairs = []
        for a, b, c in every:
            to = (a * per_plane + c) ^ k
            pairs.append((device(a, b, c), device(to // per_plane, b, to % per_plane)))
        return lax.ppermute(x, axes, pairs)

    first_pack = pack_first(query_rows, key_rows, value_rows, groups)
    first_plane = spread(swap(first_pack))
    core_index = core.astype(jnp.int32).reshape(1)
    grad_first = pack_grad(core_index, grad_out, 0, groups)
    second_pack = pack_half(query_rows, 1, groups)
    grad_second = pack_grad(core_index, grad_out, 1, groups)
    width = second_pack.shape[-1]

    plane_index = plane.astype(jnp.int32).reshape(1)
    kv_parts = relay_in(plane_index, first_plane, width)
    for k in range(1, n_plane):
        kv_parts[k] = along(kv_parts[k], k)
    second_plane = spread(swap(second_pack))
    query_parts = relay_in(plane_index, second_plane, width)
    for k in range(1, n_plane):
        query_parts[k] = along(query_parts[k], k)
    for k in range(1, groups):
        grad_first[k] = across(grad_first[k], k)
    for k in range(1, groups):
        grad_second[k] = across(grad_second[k], k)

    rows = grad_out.shape[0]
    out_first, *rows_first, carried = attend(
        table, kv_parts, None, grad_first, None, False, blocks, (groups, rows)
    )
    for k in range(1, n_plane):
        rows_first[k] = along(rows_first[k], k)
    back_first = swap(out_first)
    out_second, rows_second, main, back = attend(
        table, kv_parts, query_parts, grad_second, carried, True, blocks, (groups, rows + BLOCK)
    )
    down = [(device(a, b, c), device(a, b - 1, c)) for a, b, c in every if b]
    back = lax.ppermute(back, axes, down)
    out_second = relay_out(plane_index, rows_first, out_second)
    back_second = swap(out_second)
    rows_second = finish(core_index, rows_second, main, back)
    home_second = []
    for k in range(blocks):
        home_second.append(home(rows_second[k], k))

    attn_out = place_out(back_first)
    block_index = (plane * per_plane + part).astype(jnp.int32).reshape(1)
    grad_query, grad_key, grad_value = place_rows(block_index, home_second, groups)
    attn_out, grad_query = place_last(back_second, attn_out, grad_query)
    return (attn_out, grad_query, grad_key, grad_value)


def whole(shape, *args):
    return body(shape, *args)


def solution(mesh):
    n_seq, n_head = mesh.shape["seq"], mesh.shape["head"]
    per_plane = n_head // n_seq
    shape = (n_seq, n_seq, per_plane)
    wide = Mesh(mesh.devices.reshape(shape), ("seq", "hs", "hp"))
    rows = P(("seq", "hs", "hp"), None)
    return jax.shard_map(
        functools.partial(whole, shape),
        mesh=wide,
        in_specs=(rows, rows, rows, rows, P(), P()),
        out_specs=(rows, rows, rows, rows),
        check_vma=False,
    )
```

```python
import functools
import math

import jax
import jax.numpy as jnp
from jax import lax
from jax.experimental import pallas as pl
from jax.experimental.pallas import tpu as pltpu
from jax.sharding import Mesh
from jax.sharding import PartitionSpec as P


QH = 64
KVH = 8
DH = 128
BLOCK = 128
DOCMAX = 7
HALO = DOCMAX - 1
CHUNKS = 2

ANY = pl.BlockSpec(memory_space=pl.ANY)
NT = (((1,), (1,)), ((), ()))
F32 = jnp.float32
BF16 = jnp.bfloat16


def pack(sources, groups):
    count = sources[0][0].shape[0]
    total = sum(width for _, width, _ in sources)

    def kernel(*refs):
        ins, out_ref, held, sem_in, sem_out = refs[: len(sources)], *refs[len(sources) :]
        loads, stores = [], []
        for r in range(groups):
            at = 0
            for n, (_, width, index) in enumerate(sources):
                col = index(r) * width
                copy = pltpu.make_async_copy(
                    ins[n].at[:, col : col + width],
                    held.at[r, :, at : at + width],
                    sem_in.at[r * len(sources) + n],
                )
                copy.start()
                loads.append(copy)
                at += width
        for r in range(groups):
            for n in range(len(sources)):
                loads[r * len(sources) + n].wait()
            copy = pltpu.make_async_copy(held.at[r], out_ref.at[r], sem_out.at[r])
            copy.start()
            stores.append(copy)
        for copy in stores:
            copy.wait()

    return pl.pallas_call(
        kernel,
        in_specs=[ANY] * len(sources),
        out_specs=ANY,
        out_shape=jax.ShapeDtypeStruct((groups, count, total), BF16),
        scratch_shapes=[
            pltpu.VMEM((groups, count, total), BF16),
            pltpu.SemaphoreType.DMA((groups * len(sources),)),
            pltpu.SemaphoreType.DMA((groups,)),
        ],
        cost_estimate=pl.CostEstimate(
            flops=0, bytes_accessed=4 * groups * count * total, transcendentals=0
        ),
        compiler_params=pltpu.CompilerParams(vmem_limit_bytes=62 << 20),
    )(*[rows for rows, _, _ in sources])


def pack_first(query_rows, key_rows, value_rows, groups):
    half = QH // groups * DH // CHUNKS
    repeats = groups // KVH
    sources = [
        (query_rows, half, lambda r: r * CHUNKS),
        (key_rows, DH, lambda r: r // repeats),
        (value_rows, DH, lambda r: r // repeats),
    ]
    return pack(sources, groups)


def pack_half(rows, chunk, groups):
    half = QH // groups * DH // CHUNKS
    return pack([(rows, half, lambda r: r * CHUNKS + chunk)], groups)


def pack_grad(core_index, rows, chunk, groups):
    count = rows.shape[0]
    half = QH // groups * DH // CHUNKS

    def kernel(core_ref, in_ref, *refs):
        outs, (held, sem_in, sem_out) = refs[:groups], refs[groups:]
        loads, stores = [], []
        for k in range(groups):
            col = pl.multiple_of(((core_ref[0] ^ k) * CHUNKS + chunk) * half, half)
            copy = pltpu.make_async_copy(in_ref.at[:, pl.ds(col, half)], held.at[k], sem_in.at[k])
            copy.start()
            loads.append(copy)
        for k in range(groups):
            loads[k].wait()
            copy = pltpu.make_async_copy(held.at[k], outs[k], sem_out.at[k])
            copy.start()
            stores.append(copy)
        for copy in stores:
            copy.wait()

    return list(
        pl.pallas_call(
            kernel,
            in_specs=[pl.BlockSpec(memory_space=pltpu.SMEM), ANY],
            out_specs=[ANY] * groups,
            out_shape=[jax.ShapeDtypeStruct((count, half), BF16)] * groups,
            scratch_shapes=[
                pltpu.VMEM((groups, count, half), BF16),
                pltpu.SemaphoreType.DMA((groups,)),
                pltpu.SemaphoreType.DMA((groups,)),
            ],
            cost_estimate=pl.CostEstimate(
                flops=0, bytes_accessed=4 * groups * count * half, transcendentals=0
            ),
            compiler_params=pltpu.CompilerParams(vmem_limit_bytes=62 << 20),
            name="pack_grad",
        )(core_index, rows)
    )


def relay_in(plane_index, arrived, width):
    n_plane, per_plane, _, total = arrived.shape
    halo = total - width
    form = (per_plane, BLOCK, total + halo)
    copies = 2 if halo else 1

    def kernel(plane_ref, in_ref, *refs):
        outs, (held, sem_in, sem_out) = refs[:n_plane], refs[n_plane:]
        loads, stores = [], []
        for k in range(n_plane):
            to = plane_ref[0] ^ k
            views = [(in_ref.at[to], held.at[k, :, :, :total] if halo else held.at[k])]
            if halo:
                near = jnp.maximum(to - 1, 0)
                views.append((in_ref.at[near, :, :, width:], held.at[k, :, :, total:]))
            for n, (src, dst) in enumerate(views):
                copy = pltpu.make_async_copy(src, dst, sem_in.at[copies * k + n])
                copy.start()
                loads.append(copy)
        for k in range(n_plane):
            for copy in loads[copies * k : copies * (k + 1)]:
                copy.wait()
            copy = pltpu.make_async_copy(held.at[k], outs[k], sem_out.at[k])
            copy.start()
            stores.append(copy)
        for copy in stores:
            copy.wait()

    return list(
        pl.pallas_call(
            kernel,
            in_specs=[pl.BlockSpec(memory_space=pltpu.SMEM), ANY],
            out_specs=[ANY] * n_plane,
            out_shape=[jax.ShapeDtypeStruct(form, BF16)] * n_plane,
            scratch_shapes=[
                pltpu.VMEM((n_plane, *form), BF16),
                pltpu.SemaphoreType.DMA((copies * n_plane,)),
                pltpu.SemaphoreType.DMA((n_plane,)),
            ],
            cost_estimate=pl.CostEstimate(flops=0, bytes_accessed=4 << 20, transcendentals=0),
            compiler_params=pltpu.CompilerParams(vmem_limit_bytes=62 << 20),
            name="relay_in",
        )(plane_index, arrived)
    )


def relay_out(plane_index, parts, held):
    n_plane = len(parts)
    per_plane, _, width = parts[0].shape
    first_row = held.shape[1] - BLOCK

    def kernel(plane_ref, *refs):
        ins, (_, out_ref, buf, sem_in, sem_out) = refs[:n_plane], refs[n_plane:]
        loads, stores = [], []
        for k in range(n_plane):
            copy = pltpu.make_async_copy(ins[k], buf.at[k], sem_in.at[k])
            copy.start()
            loads.append(copy)
        for k in range(n_plane):
            loads[k].wait()
            at = (plane_ref[0] ^ k) * per_plane
            copy = pltpu.make_async_copy(
                buf.at[k], out_ref.at[pl.ds(at, per_plane), first_row:, :], sem_out.at[k]
            )
            copy.start()
            stores.append(copy)
        for copy in stores:
            copy.wait()

    return pl.pallas_call(
        kernel,
        in_specs=[pl.BlockSpec(memory_space=pltpu.SMEM)] + [ANY] * (n_plane + 1),
        out_specs=ANY,
        out_shape=jax.ShapeDtypeStruct(held.shape, BF16),
        scratch_shapes=[
            pltpu.VMEM((n_plane, per_plane, BLOCK, width), BF16),
            pltpu.SemaphoreType.DMA((n_plane,)),
            pltpu.SemaphoreType.DMA((n_plane,)),
        ],
        input_output_aliases={n_plane + 1: 0},
        cost_estimate=pl.CostEstimate(flops=0, bytes_accessed=2 << 20, transcendentals=0),
        compiler_params=pltpu.CompilerParams(vmem_limit_bytes=62 << 20),
        name="relay_out",
    )(plane_index, *parts, held)


def attend(table, kv_parts, query_parts, grad_parts, carried, last, shard_blocks, out_form):
    n_src = len(kv_parts)
    per_src = kv_parts[0].shape[0]
    blocks = shard_blocks
    width = grad_parts[0].shape[-1]
    per_core = grad_parts[0].shape[0] // BLOCK
    slots = per_core * len(grad_parts)
    owner = 2 * blocks + 2
    base = blocks - HALO
    span = blocks + HALO
    scale = 1.0 / math.sqrt(DH)
    exponent = scale * math.log2(math.e)
    first = carried is None

    def kernel(*refs):
        refs = list(refs)
        tab = refs.pop(0)
        kv_refs = [refs.pop(0) for _ in range(n_src)]
        q_refs = kv_refs if first else [refs.pop(0) for _ in range(n_src)]
        go_refs = [refs.pop(0) for _ in grad_parts]
        carried_ref = None if first else refs.pop(0)
        out_ref = refs.pop(0)
        if last:
            gq_ref, main_ref, back_ref = refs.pop(0), refs.pop(0), refs.pop(0)
        else:
            gq_refs = [refs.pop(0) for _ in range(n_src)]
            acc_out = refs.pop(0)
        qs, gs, kvs, kts, vts, acc, os, gqs, zero, sem_in, sem_go, sem_out, sem_end = refs[:13]
        if last:
            backs = refs[13]
        plane = tab[2 * blocks]
        core = tab[2 * blocks + 1]

        loads = []

        def load(src, dst):
            copy = pltpu.make_async_copy(src, dst, sem_in.at[len(loads)])
            copy.start()
            loads.append(copy)

        for k in range(n_src):
            at = (plane ^ k) * per_src
            load(kv_refs[k].at[:, :, width : width + 2 * DH], kvs.at[pl.ds(blocks + at, per_src)])
            load(kv_refs[k].at[:, :, width + 2 * DH :], kvs.at[pl.ds(at, per_src)])
            load(q_refs[k].at[:, :, :width], qs.at[pl.ds(at, per_src)])
        if not first:
            load(carried_ref, acc)

        def slot_ref(slot):
            row = pl.multiple_of(slot % per_core * BLOCK, BLOCK)
            return out_ref.at[slot // per_core, pl.ds(row, BLOCK), :]

        def go_copy(k, at, i):
            rows = go_refs[k].at[at * BLOCK : (at + 1) * BLOCK, :]
            return pltpu.make_async_copy(rows, gs.at[i], sem_go.at[i])

        def out_copy(i):
            return pltpu.make_async_copy(os.at[i], slot_ref(tab[i]), sem_out.at[i])

        for k in range(len(grad_parts)):
            for at in range(per_core):
                i = tab[owner + (core ^ k) * per_core + at]

                @pl.when(i < blocks)
                def _():
                    go_copy(k, at, i).start()

        zero[...] = jnp.zeros_like(zero)
        for slot in range(slots):
            @pl.when(tab[owner + slot] >= blocks)
            def _():
                pltpu.make_async_copy(zero, slot_ref(slot), sem_end.at[slot]).start()

        if first:
            acc[...] = jnp.zeros_like(acc)
        for copy in loads:
            copy.wait()

        @pl.loop(0, span)
        def _(b):
            at = pl.multiple_of(b * DH, DH)
            kts[:, pl.ds(at, DH)] = kvs[base + b, :, :DH].T
            vts[:, pl.ds(at, DH)] = kvs[base + b, :, DH:].T

        key_at = lax.broadcasted_iota(jnp.int32, (BLOCK, width), 0)
        query_at = lax.broadcasted_iota(jnp.int32, (BLOCK, width), 1) % BLOCK
        causal = key_at <= query_at

        def block_body(n, i, k):
            start = blocks + i - (n - 1)
            rel = HALO + i - (n - 1)
            size = n * BLOCK
            keys = kvs[pl.ds(start, n), :, :DH].reshape(size, DH)
            values = kvs[pl.ds(start, n), :, DH:].reshape(size, DH)
            lane = pl.multiple_of(rel * DH, DH)
            keys_t = kts[:, pl.ds(lane, size)]
            values_t = vts[:, pl.ds(lane, size)]
            cols = [slice(c, c + DH) for c in range(0, width, DH)]
            q_all = jnp.concatenate([qs[i, :, c] for c in cols], axis=0)
            g_all = jnp.concatenate([gs[i, :, c] for c in cols], axis=0)
            s = lax.dot_general(keys, q_all, NT, preferred_element_type=F32)
            dp = lax.dot_general(values, g_all, NT, preferred_element_type=F32)
            diag = jnp.where(causal, s[size - BLOCK :], -jnp.inf)
            s = jnp.concatenate([s[: size - BLOCK], diag], axis=0) if n > 1 else diag
            top = jnp.max(s, axis=0, keepdims=True)
            p = jnp.exp2((s - top) * exponent)
            w = p * (1.0 / jnp.sum(p, axis=0, keepdims=True))
            wb = w.astype(BF16)
            delta = jnp.sum(w * dp, axis=0, keepdims=True)
            ds = (w * (dp - delta)).astype(BF16)
            o_t = jnp.dot(values_t, wb, preferred_element_type=F32)
            dq_t = jnp.dot(keys_t, ds, preferred_element_type=F32) * scale
            dk = jnp.dot(ds, q_all, preferred_element_type=F32)
            dv = jnp.dot(wb, g_all, preferred_element_type=F32)
            acc[pl.ds(rel, n), :, :DH] += dk.reshape(n, BLOCK, DH)
            acc[pl.ds(rel, n), :, DH:] += dv.reshape(n, BLOCK, DH)
            for c in cols:
                os[i, :, c] = o_t[:, c].T.astype(BF16)
                gqs[k, :, c] = dq_t[:, c].T.astype(BF16)

        @pl.loop(0, blocks)
        def _(k):
            i = core ^ k
            go_copy(0, 0, i).wait()
            count = tab[blocks + i]
            at = k if last else ((i // per_src) ^ plane) * per_src + i % per_src
            for n in range(1, DOCMAX + 1):
                @pl.when(count == n)
                def _():
                    block_body(n, i, at)
            out_copy(i).start()

        if last:
            @pl.loop(0, HALO)
            def _(b):
                backs[b, :, :DH] = (acc[b, :, :DH] * scale).astype(BF16)
                backs[b, :, DH:] = acc[b, :, DH:].astype(BF16)

        stores = []

        def store(src, dst):
            copy = pltpu.make_async_copy(src, dst, sem_end.at[slots + len(stores)])
            copy.start()
            stores.append(copy)

        if last:
            store(backs, back_ref)
            store(gqs, gq_ref)
            store(acc.at[pl.ds(HALO, blocks)], main_ref)
        else:
            for k in range(n_src):
                store(gqs.at[pl.ds(k * per_src, per_src)], gq_refs[k])
            store(acc, acc_out)

        for copy in stores:
            copy.wait()

        @pl.loop(0, blocks)
        def _(i):
            out_copy(i).wait()

        for slot in range(slots):
            @pl.when(tab[owner + slot] >= blocks)
            def _():
                pltpu.make_async_copy(zero, slot_ref(slot), sem_end.at[slot]).wait()

    operands = [table, *kv_parts]
    if not first:
        operands += query_parts
    operands += grad_parts
    if not first:
        operands.append(carried)
    out_shape = [jax.ShapeDtypeStruct((*out_form, width), BF16)]
    if last:
        out_shape += [
            jax.ShapeDtypeStruct((blocks, BLOCK, width), BF16),
            jax.ShapeDtypeStruct((blocks, BLOCK, 2 * DH), F32),
            jax.ShapeDtypeStruct((HALO, BLOCK, 2 * DH), BF16),
        ]
    else:
        out_shape += [jax.ShapeDtypeStruct((per_src, BLOCK, width), BF16)] * n_src
        out_shape += [jax.ShapeDtypeStruct((span, BLOCK, 2 * DH), F32)]
    scratch = [
        pltpu.VMEM((blocks, BLOCK, width), BF16),
        pltpu.VMEM((blocks, BLOCK, width), BF16),
        pltpu.VMEM((2 * blocks, BLOCK, 2 * DH), BF16),
        pltpu.VMEM((DH, span * BLOCK), BF16),
        pltpu.VMEM((DH, span * BLOCK), BF16),
        pltpu.VMEM((span, BLOCK, 2 * DH), F32),
        pltpu.VMEM((blocks, BLOCK, width), BF16),
        pltpu.VMEM((blocks, BLOCK, width), BF16),
        pltpu.VMEM((BLOCK, width), BF16),
        pltpu.SemaphoreType.DMA((3 * n_src + 1,)),
        pltpu.SemaphoreType.DMA((blocks,)),
        pltpu.SemaphoreType.DMA((blocks,)),
        pltpu.SemaphoreType.DMA((slots + blocks + 3,)),
    ]
    if last:
        scratch.append(pltpu.VMEM((HALO, BLOCK, 2 * DH), BF16))
    work = blocks * width // DH * 4
    results = pl.pallas_call(
        kernel,
        in_specs=[pl.BlockSpec(memory_space=pltpu.SMEM)] + [ANY] * (len(operands) - 1),
        out_specs=[ANY] * len(out_shape),
        out_shape=out_shape,
        scratch_shapes=scratch,
        cost_estimate=pl.CostEstimate(
            flops=work * 10 * BLOCK**3, bytes_accessed=12 << 20, transcendentals=work * BLOCK**2
        ),
        compiler_params=pltpu.CompilerParams(vmem_limit_bytes=62 << 20),
        name="attend_last" if last else "attend_first",
    )(*operands)
    return results


def finish(core_index, rows, main, back):
    blocks, _, width = rows.shape
    base = blocks - HALO
    scale = 1.0 / math.sqrt(DH)

    def kernel(core_ref, rows_ref, main_ref, back_ref, *refs):
        outs, (held, mains, backs, sem_in, sem_out) = refs[:blocks], refs[blocks:]
        core = core_ref[0]
        loads = [
            pltpu.make_async_copy(main_ref, mains, sem_in.at[0]),
            pltpu.make_async_copy(back_ref, backs, sem_in.at[1]),
            pltpu.make_async_copy(rows_ref, held.at[:, :, :width], sem_in.at[2]),
        ]
        for copy in loads:
            copy.start()
        for copy in loads:
            copy.wait()
        stores = []
        for k in range(blocks):
            i = core ^ k
            near = jnp.where(i >= base, 1.0, 0.0)
            term = backs[jnp.maximum(i - base, 0)].astype(F32) * near
            held[k, :, width : width + DH] = (mains[i, :, :DH] * scale + term[:, :DH]).astype(BF16)
            held[k, :, width + DH :] = (mains[i, :, DH:] + term[:, DH:]).astype(BF16)
            copy = pltpu.make_async_copy(held.at[k], outs[k], sem_out.at[k])
            copy.start()
            stores.append(copy)
        for copy in stores:
            copy.wait()

    total = width + 2 * DH
    return pl.pallas_call(
        kernel,
        in_specs=[pl.BlockSpec(memory_space=pltpu.SMEM)] + [ANY] * 3,
        out_specs=[ANY] * blocks,
        out_shape=[jax.ShapeDtypeStruct((BLOCK, total), BF16)] * blocks,
        scratch_shapes=[
            pltpu.VMEM((blocks, BLOCK, total), BF16),
            pltpu.VMEM((blocks, BLOCK, 2 * DH), F32),
            pltpu.VMEM((HALO, BLOCK, 2 * DH), BF16),
            pltpu.SemaphoreType.DMA((3,)),
            pltpu.SemaphoreType.DMA((blocks,)),
        ],
        cost_estimate=pl.CostEstimate(flops=0, bytes_accessed=5 << 20, transcendentals=0),
        compiler_params=pltpu.CompilerParams(vmem_limit_bytes=62 << 20),
        name="finish",
    )(core_index, rows, main, back)


def place_last(block_index, last_rows, parts, out, groups):
    repeats = groups // KVH
    _, total, half = parts.shape
    width = 2 * half
    rows = total - BLOCK

    def kernel(*refs):
        at_ref, *refs = refs
        lasts, refs = refs[:groups], refs[groups:]
        in_ref, _, out_ref, gq_ref, gk_ref, gv_ref, buf, ends, held, sums, sem_in, sem_out = refs
        at = at_ref[0]
        loads, stores = [], []

        def load(src, dst):
            copy = pltpu.make_async_copy(src, dst, sem_in.at[len(loads)])
            copy.start()
            loads.append(copy)

        def store(src, dst):
            copy = pltpu.make_async_copy(src, dst, sem_out.at[len(stores)])
            copy.start()
            stores.append(copy)

        for k in range(groups):
            load(lasts[k].at[:, half:], held.at[at ^ k])
        for k in range(groups):
            load(lasts[k].at[:, :half], ends.at[k])
        for r in range(groups):
            load(in_ref.at[r], buf.at[r])
        for k in range(groups):
            loads[k].wait()
        for head in range(KVH):
            term = held[head * repeats].astype(F32)
            for extra in range(1, repeats):
                term += held[head * repeats + extra].astype(F32)
            sums[0, :, head * DH : (head + 1) * DH] = term[:, :DH].astype(BF16)
            sums[1, :, head * DH : (head + 1) * DH] = term[:, DH:].astype(BF16)
        store(sums.at[0], gk_ref)
        store(sums.at[1], gv_ref)
        for k in range(groups):
            col = pl.multiple_of((at ^ k) * width + half, half)
            loads[groups + k].wait()
            store(ends.at[k], gq_ref.at[:, pl.ds(col, half)])
        for r in range(groups):
            first, second = 2 * r * half, (2 * r + 1) * half
            loads[2 * groups + r].wait()
            store(buf.at[r, :rows, :], out_ref.at[:, second : second + half])
            store(buf.at[r, rows:, :], gq_ref.at[:, first : first + half])
        for copy in stores:
            copy.wait()

    return pl.pallas_call(
        kernel,
        in_specs=[pl.BlockSpec(memory_space=pltpu.SMEM)] + [ANY] * (groups + 2),
        out_specs=[ANY] * 4,
        out_shape=[
            jax.ShapeDtypeStruct(out.shape, BF16),
            jax.ShapeDtypeStruct((BLOCK, QH * DH), BF16),
            jax.ShapeDtypeStruct((BLOCK, KVH * DH), BF16),
            jax.ShapeDtypeStruct((BLOCK, KVH * DH), BF16),
        ],
        scratch_shapes=[
            pltpu.VMEM((groups, total, half), BF16),
            pltpu.VMEM((groups, BLOCK, half), BF16),
            pltpu.VMEM((groups, BLOCK, 2 * DH), BF16),
            pltpu.VMEM((2, BLOCK, KVH * DH), BF16),
            pltpu.SemaphoreType.DMA((3 * groups,)),
            pltpu.SemaphoreType.DMA((3 * groups + 2,)),
        ],
        input_output_aliases={groups + 2: 0},
        cost_estimate=pl.CostEstimate(flops=0, bytes_accessed=10 << 20, transcendentals=0),
        compiler_params=pltpu.CompilerParams(vmem_limit_bytes=62 << 20),
        name="place_last",
    )(block_index, *last_rows, parts, out)


def place_out(parts):
    groups, rows, half = parts.shape

    def kernel(in_ref, out_ref, buf, sem_in, sem_out):
        loads = [pltpu.make_async_copy(in_ref.at[r], buf.at[r], sem_in.at[r]) for r in range(groups)]
        stores = []
        for copy in loads:
            copy.start()
        for r in range(groups):
            col = CHUNKS * r * half
            loads[r].wait()
            copy = pltpu.make_async_copy(buf.at[r], out_ref.at[:, col : col + half], sem_out.at[r])
            copy.start()
            stores.append(copy)
        for copy in stores:
            copy.wait()

    return pl.pallas_call(
        kernel,
        in_specs=[ANY],
        out_specs=ANY,
        out_shape=jax.ShapeDtypeStruct((rows, QH * DH), BF16),
        scratch_shapes=[
            pltpu.VMEM((groups, rows, half), BF16),
            pltpu.SemaphoreType.DMA((groups,)),
            pltpu.SemaphoreType.DMA((groups,)),
        ],
        cost_estimate=pl.CostEstimate(
            flops=0, bytes_accessed=4 * groups * rows * half, transcendentals=0
        ),
        compiler_params=pltpu.CompilerParams(vmem_limit_bytes=62 << 20),
        name="place_out",
    )(parts)


def body(shape, query_rows, key_rows, value_rows, grad_out, doc_ids, route_table):
    n_seq, n_plane, per_plane = shape
    groups = n_seq * per_plane
    blocks = n_plane * per_plane
    slots = route_table.shape[1] * route_table.shape[2]
    axes = ("seq", "hs", "hp")
    plane_axes = ("seq", "hp")
    seq_at = lax.axis_index("seq")
    plane = lax.axis_index("hs")
    part = lax.axis_index("hp")
    core = seq_at * per_plane + part

    def device(seq, hs, hp):
        return (seq * n_plane + hs) * per_plane + hp

    every = [(a, b, c) for a in range(n_seq) for b in range(n_plane) for c in range(per_plane)]

    def swap(x):
        return lax.all_to_all(x, plane_axes, split_axis=0, concat_axis=0, tiled=True)

    def along(x, k):
        return lax.ppermute(x, axes, [(device(a, b, c), device(a, b ^ k, c)) for a, b, c in every])

    def home(x, k):
        pairs = []
        for a, b, c in every:
            index = (a * per_plane + c) ^ k
            pairs.append((device(a, b, c), device(b, index // per_plane, index % per_plane)))
        return lax.ppermute(x, axes, pairs)

    routes = lax.dynamic_index_in_dim(route_table, plane, 0, keepdims=False).reshape(slots)
    match = routes[None, :] == jnp.arange(blocks, dtype=jnp.int32)[:, None]
    slot_of = jnp.sum(jnp.where(match, jnp.arange(slots, dtype=jnp.int32)[None, :], 0), axis=1)
    docs_pad = jnp.concatenate([jnp.full((HALO,), -1, jnp.int32), doc_ids])
    docs = lax.dynamic_slice_in_dim(docs_pad, plane * blocks, blocks + HALO, 0)
    own = docs[HALO:]
    counts = sum(
        (docs[HALO - d : HALO - d + blocks] == own).astype(jnp.int32) for d in range(DOCMAX)
    )
    table = jnp.concatenate([slot_of, counts, jnp.stack([plane, core]).astype(jnp.int32), routes])

    def spread(x):
        return x.reshape((n_seq, per_plane) + x.shape[1:])

    def across(x, k):
        pairs = []
        for a, b, c in every:
            to = (a * per_plane + c) ^ k
            pairs.append((device(a, b, c), device(to // per_plane, b, to % per_plane)))
        return lax.ppermute(x, axes, pairs)

    first_pack = pack_first(query_rows, key_rows, value_rows, groups)
    first_plane = spread(swap(first_pack))
    core_index = core.astype(jnp.int32).reshape(1)
    grad_first = pack_grad(core_index, grad_out, 0, groups)
    second_pack = pack_half(query_rows, 1, groups)
    grad_second = pack_grad(core_index, grad_out, 1, groups)
    width = second_pack.shape[-1]

    plane_index = plane.astype(jnp.int32).reshape(1)
    kv_parts = relay_in(plane_index, first_plane, width)
    for k in range(1, n_plane):
        kv_parts[k] = along(kv_parts[k], k)
    second_plane = spread(swap(second_pack))
    query_parts = relay_in(plane_index, second_plane, width)
    for k in range(1, n_plane):
        query_parts[k] = along(query_parts[k], k)
    for k in range(1, groups):
        grad_first[k] = across(grad_first[k], k)
    for k in range(1, groups):
        grad_second[k] = across(grad_second[k], k)

    rows = grad_out.shape[0]
    out_first, *rows_first, carried = attend(
        table, kv_parts, None, grad_first, None, False, blocks, (groups, rows)
    )
    for k in range(1, n_plane):
        rows_first[k] = along(rows_first[k], k)
    back_first = swap(out_first)
    out_second, rows_second, main, back = attend(
        table, kv_parts, query_parts, grad_second, carried, True, blocks, (groups, rows + BLOCK)
    )
    down = [(device(a, b, c), device(a, b - 1, c)) for a, b, c in every if b]
    back = lax.ppermute(back, axes, down)
    out_second = relay_out(plane_index, rows_first, out_second)
    back_second = swap(out_second)
    rows_second = finish(core_index, rows_second, main, back)
    home_second = []
    for k in range(blocks):
        home_second.append(home(rows_second[k], k))

    attn_out = place_out(back_first)
    block_index = (plane * per_plane + part).astype(jnp.int32).reshape(1)
    attn_out, grad_query, grad_key, grad_value = place_last(
        block_index, home_second, back_second, attn_out, groups
    )
    return (attn_out, grad_query, grad_key, grad_value)


def whole(shape, *args):
    return body(shape, *args)


def solution(mesh):
    n_seq, n_head = mesh.shape["seq"], mesh.shape["head"]
    per_plane = n_head // n_seq
    shape = (n_seq, n_seq, per_plane)
    wide = Mesh(mesh.devices.reshape(shape), ("seq", "hs", "hp"))
    rows = P(("seq", "hs", "hp"), None)
    return jax.shard_map(
        functools.partial(whole, shape),
        mesh=wide,
        in_specs=(rows, rows, rows, rows, P(), P()),
        out_specs=(rows, rows, rows, rows),
        check_vma=False,
    )
```
